256 devices in a mesh: dp: 8 (over x, core), seq: 32 (over z, y).
Axes of the slice: x: 4, y: 4, z: 8, core: 2. Of those that a mesh axis runs over, the one named last changes fastest.
Arguments:
- features: bfloat16 [8, 4096, 2048], P('dp', 'seq'), may hold values from -6 to 6
- queries: bfloat16 [8, 4096, 2048], P('dp', 'seq'), may hold values from -4.5 to 4.5
- key_rows: bfloat16 [8, 4096, 2048], P('dp', 'seq'), may hold values from -4.5 to 4.5
- value_rows: bfloat16 [8, 4096, 2048], P('dp', 'seq'), may hold values from -6 to 6
- cotangent: bfloat16 [8, 4096, 2048], P('dp', 'seq'), may hold values from -6 to 6
- global_queries: bfloat16 [8, 64, 2048], P('dp'), may hold values from -4.5 to 4.5
- global_keys: bfloat16 [8, 64, 2048], P('dp'), may hold values from -4.5 to 4.5
- global_values: bfloat16 [8, 64, 2048], P('dp'), may hold values from -6 to 6
- random_blocks: int32 [8, 64, 3], P('dp'), may hold values from 0 to 63, as said below
Outputs:
- attended: bfloat16 [8, 4096, 2048], P('dp', 'seq')
- global_attended: bfloat16 [8, 64, 2048], P('dp')
- weight_grad: float32 [2048, 2048], P(('dp', 'seq'))
The draws below stay inside these ranges and needn't reach their ends.
Inputs may be any that keep to these rules, and one draw needn't show every extreme that they name: `random_blocks`: block b of a document lies on seq device b // 2. The 6 random blocks named by the 2 query blocks of one device lie on 6 different devices.
All inputs are finite; a program needn't handle non-finite values.
Results may differ from the reference program's by a relative error of at most 0.025.
Values may be sent and summed in bfloat16 or wider, within the bound.
A program may use at most 192 MiB of HBM per device.

```python
import math
import jax
import jax.numpy as jnp
from jax import lax

D_WIN = 2048
HEADS = 16
HEAD_DIM = 128
G = 64
BLOCK = 64
R = 3
TOK_DEV = 128
HD = 2048
DOCS = 8
LENGTH = 4096
NBLK = 64
BLK_DEV = 2
REQ = 6
N_SEQ = 32


def drawn_field(key, rows, want_keys):
    base_key = jax.random.fold_in(key, 7)
    query_key, key_key = jax.random.split(base_key, 2)
    own_key = key_key if want_keys else query_key
    shape = (DOCS, rows, HD)
    field = jnp.clip(jax.random.normal(own_key, shape, jnp.float32), -4.5, 4.5)
    return field.astype(jnp.bfloat16)


def draw_queries(key, part):
    return drawn_field(key, LENGTH, False)


def draw_key_rows(key, part):
    return drawn_field(key, LENGTH, True)


def draw_global_queries(key, part):
    return drawn_field(jax.random.fold_in(key, 19), G, False)


def draw_global_keys(key, part):
    return drawn_field(jax.random.fold_in(key, 19), G, True)


def draw_random_blocks(key, part):
    devices = NBLK // BLK_DEV
    hot_key, noise_key, within_key = jax.random.split(jax.random.fold_in(key, 3), 3)
    hotness = jax.random.randint(hot_key, (DOCS, 1, devices), 0, 3)
    noise = jax.random.randint(noise_key, (DOCS, devices, devices), 0, devices)
    ranking = (noise - devices * hotness) * devices + jnp.arange(devices)[None, None, :]
    owner_order = jnp.argsort(ranking, axis=-1, stable=True)
    request_slot = jnp.arange(REQ) % devices
    owners = owner_order[:, :, request_slot]
    within = jax.random.randint(within_key, (DOCS, devices, REQ), 0, BLK_DEV)
    block_ids = owners * BLK_DEV + within
    return block_ids.reshape(DOCS, NBLK, R).astype(jnp.int32)


def with_spikes(drawn, key, source, target, shards_of, factor):
    owner, partner = [(jnp.arange(drawn.shape[axis_at]) // (drawn.shape[axis_at] // shards_of)).reshape([-1 if axis == axis_at else 1 for axis in range(drawn.ndim)]) for axis_at in (source, target)]
    chosen = jax.random.permutation(key, shards_of)[partner]
    strong = (owner == chosen) | (owner == (partner + shards_of // 2) % shards_of)
    return jnp.where(strong, factor * drawn, drawn)


def block_scale(stream_key, shape, cuts, smallest, top_value):
    level, own = 1.0, jax.random.fold_in(stream_key, 6)
    for axis_at, blocks in cuts:
        heights = jnp.exp(jax.random.uniform(jax.random.fold_in(own, axis_at), (blocks,), jnp.float32, smallest / len(cuts), top_value / len(cuts)))
        level = level * jnp.repeat(heights, shape[axis_at] // blocks).reshape([-1 if axis == axis_at else 1 for axis in range(len(shape))])
    return level


def normal_values(stream_key, dims, scale, bound, pieces=(), dtype=jnp.bfloat16):
    drawn = jax.random.normal(stream_key, dims, jnp.float32) * scale
    if len(pieces) > 0:
        drawn = block_scale(stream_key, dims, pieces, -0.22, 0.18) * drawn
    return jnp.clip(drawn, min=-bound, max=bound).astype(dtype)


def bell_draw_with(key, extent, spread, limit, cuts, heavy, kind=jnp.bfloat16):
    result = spread * jax.random.normal(key, extent, jnp.float32)
    if cuts:
        result = result * block_scale(key, extent, cuts, -0.22, 0.18)
    return jnp.clip(with_spikes(result, jax.random.fold_in(key, 3), *heavy), -limit, limit).astype(kind)


def setup_inputs(seed: int = 0) -> dict:
    splits = jax.random.split(jax.random.key(seed), 10)
    return {
        "features": bell_draw_with(splits[0], (DOCS, LENGTH, D_WIN), 1.0, 6.0, ((0, 8), (1, 32)), (1, 2, 32, 2.75)),
        "queries": draw_queries(jax.random.fold_in(splits[9], 71), 0),
        "key_rows": draw_key_rows(jax.random.fold_in(splits[9], 71), 0),
        "value_rows": normal_values(splits[3], (DOCS, LENGTH, HD), 1.0, 6.0, ((0, 8), (1, 32))),
        "cotangent": normal_values(splits[4], (DOCS, LENGTH, HD), 1.0, 6.0, ((0, 8), (1, 32))),
        "global_queries": draw_global_queries(jax.random.fold_in(splits[9], 71), 0),
        "global_keys": draw_global_keys(jax.random.fold_in(splits[9], 71), 0),
        "global_values": normal_values(splits[7], (DOCS, G, HD), 1.0, 6.0, ((0, 8),)),
        "random_blocks": draw_random_blocks(jax.random.fold_in(splits[9], 71), 0),
    }


NEGATIVE = -1e+30

def to_float(array):
    return array.astype(jnp.float32)

def span_partial(global_heads, span_keys, span_values, scaling):
    scores = jnp.einsum('ghe,the->hgt', global_heads, span_keys) * scaling
    peak_score = lax.optimization_barrier(jnp.max(scores, axis=-1))
    exp_weights = jnp.exp(scores - peak_score[..., None])
    total_mass = lax.optimization_barrier(jnp.sum(exp_weights, axis=-1))
    value_part = jnp.einsum('hgt,the->ghe', to_float(exp_weights.astype(jnp.bfloat16)), span_values)
    return (peak_score, total_mass, value_part)

def global_document(global_queries, key_rows, value_rows, global_keys, global_values, scaling):
    global_heads = to_float(global_queries).reshape(G, HEADS, HEAD_DIM)
    span_keys = to_float(key_rows).reshape(N_SEQ, TOK_DEV, HEADS, HEAD_DIM)
    span_values = to_float(value_rows).reshape(N_SEQ, TOK_DEV, HEADS, HEAD_DIM)

    def one_span(span_inputs):
        return span_partial(global_heads, span_inputs[0], span_inputs[1], scaling)
    peaks, masses, parts = lax.map(one_span, (span_keys, span_values))
    own_peak, own_mass, own_part = span_partial(global_heads, to_float(global_keys).reshape(G, HEADS, HEAD_DIM), to_float(global_values).reshape(G, HEADS, HEAD_DIM), scaling)
    top_score = jnp.maximum(lax.optimization_barrier(jnp.max(peaks, axis=0)), own_peak)
    span_weight = jnp.exp(peaks - top_score[None])
    own_weight = jnp.exp(own_peak - top_score)
    total_mass = lax.optimization_barrier(jnp.sum(masses * span_weight, axis=0)) + own_mass * own_weight
    value_sum = lax.optimization_barrier(jnp.sum(parts * jnp.transpose(span_weight, (0, 2, 1))[..., None], axis=0))
    value_sum = value_sum + own_part * own_weight.T[..., None]
    return (value_sum / total_mass.T[..., None]).reshape(G, HD).astype(jnp.bfloat16)

def long_document(queries, key_rows, value_rows, cotangent, global_keys, global_values, random_blocks, scaling):
    query_blocks = to_float(queries).reshape(NBLK, BLOCK, HEADS, HEAD_DIM)
    zero_block = jnp.zeros((1, BLOCK, HEADS, HEAD_DIM), jnp.float32)

    def windows(source):
        blocks = to_float(source).reshape(NBLK, BLOCK, HEADS, HEAD_DIM)
        padded = jnp.concatenate([zero_block, blocks, zero_block], axis=0)
        return jnp.concatenate([padded[:-2], padded[1:-1], padded[2:]], axis=1)

    def randoms(source):
        blocks = to_float(source).reshape(NBLK, BLOCK, HEADS, HEAD_DIM)
        return blocks[random_blocks].reshape(NBLK, R * BLOCK, HEADS, HEAD_DIM)
    window_keys = windows(key_rows)
    window_values = windows(value_rows)
    random_keys = randoms(key_rows)
    random_values = randoms(value_rows)
    glob_keys = to_float(global_keys).reshape(G, HEADS, HEAD_DIM)
    glob_values = to_float(global_values).reshape(G, HEADS, HEAD_DIM)
    block_number = jnp.arange(NBLK)[:, None]
    column = jnp.arange(3 * BLOCK)[None, :]
    valid_keys = ((column >= BLOCK) | (block_number > 0)) & ((column < 2 * BLOCK) | (block_number < NBLK - 1))
    window_scores = jnp.einsum('bqhe,bkhe->bhqk', query_blocks, window_keys) * scaling
    window_scores = jnp.where(valid_keys[:, None, None, :], window_scores, NEGATIVE)
    random_scores = jnp.einsum('bqhe,bkhe->bhqk', query_blocks, random_keys) * scaling
    global_scores = jnp.einsum('bqhe,khe->bhqk', query_blocks, glob_keys) * scaling
    scores = jnp.concatenate([window_scores, random_scores, global_scores], axis=-1)
    peak_score = lax.optimization_barrier(jnp.max(scores, axis=-1, keepdims=True))
    exp_weights = jnp.exp(scores - peak_score)
    soft_weights = exp_weights / lax.optimization_barrier(jnp.sum(exp_weights, axis=-1, keepdims=True))
    low_weights = to_float(soft_weights.astype(jnp.bfloat16))
    split_one = 3 * BLOCK
    split_two = 3 * BLOCK + R * BLOCK
    combined = jnp.einsum('bhqk,bkhe->bqhe', low_weights[..., :split_one], window_values)
    combined = combined + jnp.einsum('bhqk,bkhe->bqhe', low_weights[..., split_one:split_two], random_values)
    combined = combined + jnp.einsum('bhqk,khe->bqhe', low_weights[..., split_two:], glob_values)
    attended = combined.reshape(LENGTH, HD).astype(jnp.bfloat16)
    grad_blocks = to_float(cotangent).reshape(NBLK, BLOCK, HEADS, HEAD_DIM)
    delta_rows = lax.optimization_barrier(jnp.sum(grad_blocks * to_float(attended).reshape(NBLK, BLOCK, HEADS, HEAD_DIM), axis=-1))
    grad_weights = jnp.concatenate([jnp.einsum('bqhe,bkhe->bhqk', grad_blocks, window_values), jnp.einsum('bqhe,bkhe->bhqk', grad_blocks, random_values), jnp.einsum('bqhe,khe->bhqk', grad_blocks, glob_values)], axis=-1)
    grad_scores = soft_weights * (grad_weights - jnp.transpose(delta_rows, (0, 2, 1))[..., None])
    grad_scores = to_float(grad_scores.astype(jnp.bfloat16))
    grad_query = jnp.einsum('bhqk,bkhe->bqhe', grad_scores[..., :split_one], window_keys)
    grad_query = grad_query + jnp.einsum('bhqk,bkhe->bqhe', grad_scores[..., split_one:split_two], random_keys)
    grad_query = grad_query + jnp.einsum('bhqk,khe->bqhe', grad_scores[..., split_two:], glob_keys)
    query_grad = (grad_query * scaling).reshape(LENGTH, HD).astype(jnp.bfloat16)
    return (attended, query_grad)

def reference(features, queries, key_rows, value_rows, cotangent, global_queries, global_keys, global_values, random_blocks):
    scaling = 1.0 / math.sqrt(HEAD_DIM)

    def per_document(weight_sum, inputs):
        doc_features, doc_queries, doc_keys, doc_values, doc_cotangent, global_query_doc, global_key_doc, global_value_doc, random_doc = inputs
        attended, query_grad = long_document(doc_queries, doc_keys, doc_values, doc_cotangent, global_key_doc, global_value_doc, random_doc, scaling)
        global_attended = global_document(global_query_doc, doc_keys, doc_values, global_key_doc, global_value_doc, scaling)
        weight_sum = weight_sum + jnp.dot(doc_features.T, query_grad, preferred_element_type=jnp.float32)
        return (weight_sum, (attended, global_attended))
    initial = jnp.zeros((D_WIN, HD), jnp.float32)
    weight_grad, (attended, global_attended) = lax.scan(per_document, initial, (features, queries, key_rows, value_rows, cotangent, global_queries, global_keys, global_values, random_blocks))
    return (attended, global_attended, weight_grad)
```

```python
import functools
import math

import jax
import jax.numpy as jnp
from jax import lax
from jax.experimental import pallas as pl
from jax.experimental.pallas import tpu as pltpu
from jax.sharding import PartitionSpec as P

E = 128
BLOCK = 64
R = 3
NY = 4
NC = 2
NEGATIVE = -1e30
MESH = pl.DeviceIdType.MESH
ANY = pl.BlockSpec(memory_space=pl.ANY)


def place(seqs):
    d, s = lax.axis_index("dp"), lax.axis_index("seq")
    return d, s, d // NC, d % NC, s // NY, s % NY


def head_columns(h):
    return pl.ds(pl.multiple_of(h * E, E), E)


def remote(src, dst, send, recv, d, s):
    return pltpu.make_async_remote_copy(
        src_ref=src, dst_ref=dst, send_sem=send, recv_sem=recv, device_id=(d, s), device_id_type=MESH
    )


def signal(sem, d, s):
    pl.semaphore_signal(sem, inc=1, device_id=(d, s), device_id_type=MESH)


def shuffle_kernel(seqs, xs, *refs):
    q, k, v, g, f, gq, gk, gv, rb = refs[:9]
    qo, ko, vo, go, fo, gqo, gko, gvo, rbo = refs[9:18]
    a_send, a_recv, b_send, b_recv, f_send, f_recv, c_send, c_recv = refs[18:]
    d, s, x, c, z, y = place(seqs)
    half = seqs // 2
    heads = half
    tokens = s // half
    slot = s % half
    sibling = x * NC + (1 - c)
    owner = z % NC
    mine = jnp.logical_and(owner == c, tokens == c)

    barrier = pltpu.get_barrier_semaphore()

    def greet(i, carry):
        source = c * half + i

        @pl.when(jnp.logical_not(jnp.logical_and(owner == c, source == s)))
        def _():
            signal(barrier, x * NC + owner, source)

        return carry

    lax.fori_loop(0, half, greet, 0)
    signal(barrier, sibling, s)

    def greet_f(i, carry):
        to_x, to_y = (x + i // NY) % xs, (y + i) % NY
        signal(barrier, to_x * NC + c, z * NY + to_y)
        return carry

    lax.fori_loop(1, xs * NY, greet_f, 0)

    @pl.when(mine)
    def _():
        pl.semaphore_wait(barrier, half + xs * NY - 1)

    @pl.when(jnp.logical_not(mine))
    def _():
        pl.semaphore_wait(barrier, half + xs * NY)

    def target(i):
        h = (i + s) % heads
        return h, ((h // NY) * NC + c) * NY + h % NY

    def pieces(h):
        columns = head_columns(h)
        return (
            (k.at[0, :, columns], ko.at[s]),
            (v.at[0, :, columns], vo.at[s]),
            (q.at[0, :, columns], qo.at[slot]),
            (g.at[0, :, columns], go.at[slot]),
        )

    def send(n):
        def body(i, carry):
            h, to = target(i)
            src, dst = pieces(h)[n]
            here = jnp.logical_and(mine, to == s)

            @pl.when(here)
            def _():
                pltpu.make_async_copy(src, dst, a_recv.at[n]).start()

            @pl.when(jnp.logical_not(here))
            def _():
                remote(src, dst, a_send.at[n], a_recv.at[n], x * NC + tokens, to).start()

            return carry

        lax.fori_loop(0, heads, body, 0)

    send(0)
    send(1)

    my_head = (z // NC) * NY + y
    columns = head_columns(my_head)
    rows = gqo.shape[0]
    shared = (
        (gq.at[0, pl.ds(pl.multiple_of(c * rows, rows), rows), columns],
         gq.at[0, pl.ds(pl.multiple_of((1 - c) * rows, rows), rows), columns], gqo),
        (gk.at[0, :, columns], gk.at[0, :, columns], gko),
        (gv.at[0, :, columns], gv.at[0, :, columns], gvo),
        (rb.at[0], rb.at[0], rbo),
    )

    @pl.when(owner == c)
    def _():
        for n, (own, other, dst) in enumerate(shared):
            pltpu.make_async_copy(own, dst, c_recv.at[n]).start()
            remote(other, dst, c_send.at[n], c_recv.at[n], sibling, s).start()

    send(2)
    send(3)

    width = fo.shape[2]

    def send_f(i, carry):
        to_x, to_y = (x + i // NY) % xs, (y + i) % NY
        src = f.at[0, :, pl.ds(pl.multiple_of(to_x * width, width), width)]
        remote(src, fo.at[x * NY + y], f_send, f_recv, to_x * NC + c, z * NY + to_y).start()
        return carry

    src = f.at[0, :, pl.ds(pl.multiple_of(x * width, width), width)]
    pltpu.make_async_copy(src, fo.at[x * NY + y], f_recv).start()
    lax.fori_loop(1, xs * NY, send_f, 0)

    def arrived(ref, sem):
        pltpu.make_async_copy(ref, ref, sem).wait()

    part = pl.ds(pl.multiple_of(c * half, half), half)
    other_part = pl.ds(pl.multiple_of((1 - c) * half, half), half)
    for n, out in enumerate((ko, vo)):
        arrived(out.at[part], a_recv.at[n])
        remote(out.at[part], out.at[part], b_send.at[n], b_recv.at[n], sibling, s).start()
    arrived(qo, a_recv.at[2])
    arrived(go, a_recv.at[3])
    for n, out in enumerate((ko, vo)):
        arrived(out.at[other_part], b_recv.at[n])
    for n, (_, _, dst) in enumerate(shared):
        arrived(dst, c_recv.at[n])
    arrived(fo, f_recv)

    for n in range(4):
        @pl.when(mine)
        def _():
            arrived(qo.at[pl.ds(0, half - 1)], a_send.at[n])

        @pl.when(jnp.logical_not(mine))
        def _():
            arrived(qo, a_send.at[n])
    for n, out in enumerate((ko, vo)):
        arrived(out.at[part], b_send.at[n])

    @pl.when(owner == c)
    def _():
        for n, (_, _, dst) in enumerate(shared):
            arrived(dst, c_send.at[n])

    arrived(fo.at[pl.ds(0, xs * NY - 1)], f_send)


def shuffle(seqs, xs, q, k, v, g, f, gq, gk, gv, rb):
    tokens, wide = q.shape[1], f.shape[2]
    half = seqs // 2
    bf16 = jnp.bfloat16
    shape = jax.ShapeDtypeStruct
    outs = (
        shape((half, tokens, E), bf16),
        shape((seqs, tokens, E), bf16),
        shape((seqs, tokens, E), bf16),
        shape((half, tokens, E), bf16),
        shape((xs * NY, tokens, wide // xs), bf16),
        shape((gq.shape[1] // NC, E), bf16),
        shape((gk.shape[1], E), bf16),
        shape((gv.shape[1], E), bf16),
        shape(rb.shape[1:], jnp.int32),
    )
    dma = pltpu.SemaphoreType.DMA
    return pl.pallas_call(
        functools.partial(shuffle_kernel, seqs, xs),
        out_shape=outs,
        in_specs=[ANY] * 9,
        out_specs=[ANY] * 9,
        scratch_shapes=[dma((4,)), dma((4,)), dma((2,)), dma((2,)), dma, dma, dma((4,)), dma((4,))],
        compiler_params=pltpu.CompilerParams(collective_id=0, has_side_effects=True),
        name="shuffle",
    )(q, k, v, g, f, gq, gk, gv, rb)


def attention_kernel(blocks, rb, q, k, v, g, gq, gk, gv, att, grad, gatt):
    scaling = 1.0 / math.sqrt(E)
    count = q.shape[0] // BLOCK
    c = lax.axis_index("dp") % NC
    dot = functools.partial(lax.dot_general, preferred_element_type=jnp.float32)
    nt = (((1,), (1,)), ((), ()))
    nn = (((1,), (0,)), ((), ()))
    g_k, g_v = gk[...], gv[...]
    columns = 3 * BLOCK + R * BLOCK + g_k.shape[0]

    def rows(b):
        return pl.ds(pl.multiple_of(b * BLOCK, BLOCK), BLOCK)

    def block(i, carry):
        b = c * count + i
        first = jnp.clip(b - 1, 0, blocks - 3)
        window = pl.ds(pl.multiple_of(first * BLOCK, BLOCK), 3 * BLOCK)
        picks = [rows(rb[b, n]) for n in range(R)]
        keys = jnp.concatenate([k[window, :]] + [k[p, :] for p in picks] + [g_k], axis=0)
        values = jnp.concatenate([v[window, :]] + [v[p, :] for p in picks] + [g_v], axis=0)
        q_b, g_b = q[rows(i), :], g[rows(i), :]
        scores = dot(q_b, keys, nt) * scaling
        low = jnp.where(b == blocks - 1, BLOCK, 0)
        high = jnp.where(b == 0, 2 * BLOCK, 3 * BLOCK)
        column = lax.broadcasted_iota(jnp.int32, (BLOCK, columns), 1)
        valid = (column >= low) & ((column < high) | (column >= 3 * BLOCK))
        scores = jnp.where(valid, scores, NEGATIVE)
        peak = jnp.max(scores, axis=-1, keepdims=True)
        weights = jnp.exp(scores - peak)
        probs = weights / jnp.sum(weights, axis=-1, keepdims=True)
        attended = dot(probs.astype(jnp.bfloat16), values, nn).astype(jnp.bfloat16)
        delta = jnp.sum(
            g_b.astype(jnp.float32) * attended.astype(jnp.float32), axis=-1, keepdims=True
        )
        dprobs = dot(g_b, values, nt)
        dscores = (probs * (dprobs - delta)).astype(jnp.bfloat16)
        att[rows(i), :] = attended
        grad[rows(i), :] = (dot(dscores, keys, nn) * scaling).astype(jnp.bfloat16)
        return carry

    lax.fori_loop(0, count, block, 0, unroll=2)

    g_q = gq[...]
    long_scores = dot(g_q, k[...], nt) * scaling
    own_scores = dot(g_q, g_k, nt) * scaling
    peak = jnp.maximum(
        jnp.max(long_scores, axis=-1, keepdims=True), jnp.max(own_scores, axis=-1, keepdims=True)
    )
    long_weights = jnp.exp(long_scores - peak)
    own_weights = jnp.exp(own_scores - peak)
    mass = jnp.sum(long_weights, axis=-1, keepdims=True) + jnp.sum(own_weights, axis=-1, keepdims=True)
    total = dot(long_weights.astype(jnp.bfloat16), v[...], nn)
    total = total + dot(own_weights.astype(jnp.bfloat16), g_v, nn)
    gatt[...] = (total / mass).astype(jnp.bfloat16)


def attention(q, k, v, g, gq, gk, gv, rb):
    flat = [a.reshape(-1, E) for a in (q, k, v, g)]
    shape = jax.ShapeDtypeStruct
    vmem = pl.BlockSpec(memory_space=pltpu.VMEM)
    return pl.pallas_call(
        functools.partial(attention_kernel, flat[1].shape[0] // BLOCK),
        out_shape=(
            shape(flat[0].shape, jnp.bfloat16),
            shape(flat[0].shape, jnp.bfloat16),
            shape(gq.shape, jnp.bfloat16),
        ),
        in_specs=[pl.BlockSpec(memory_space=pltpu.SMEM)] + [vmem] * 7,
        out_specs=[vmem] * 3,
        compiler_params=pltpu.CompilerParams(vmem_limit_bytes=40 << 20),
        name="attention",
    )(rb, *flat, gq, gk, gv)


def product_kernel(seqs, xs, *refs):
    att, grad, gatt, f = refs[:4]
    att_o, gatt_o, w_o = refs[4:7]
    (f_v, grads, total, from_sibling, part, pieces,
     o_send, o_recv, g_send, g_recv, n_send, n_recv, x_send, x_recv,
     s_send, s_recv, w_send, w_recv, f_sem) = refs[7:]
    d, s, x, c, z, y = place(seqs)
    half = seqs // 2
    tokens = att_o.shape[0]
    owner = z % NC
    sibling = x * NC + (1 - c)
    doc = x * NC + owner
    head = (z // NC) * NY + y
    rows_z = half // NY
    mine = jnp.logical_and(owner == c, z // rows_z == c)

    load = pltpu.make_async_copy(f, f_v, f_sem)
    load.start()

    barrier = pltpu.get_barrier_semaphore()

    def greet(i, carry):
        from_z = (i // NY) * NC + c
        from_s = from_z * NY + i % NY
        for t in range(NC):
            @pl.when(jnp.logical_not(jnp.logical_and(from_s == s, c == t)))
            def _():
                signal(barrier, x * NC + t, from_s)

        return carry

    lax.fori_loop(0, half, greet, 0)
    signal(barrier, sibling, s)
    lax.fori_loop(1, xs, lambda i, a: (signal(barrier, ((x + i) % xs) * NC + c, s), a)[1], 0)
    lax.fori_loop(1, seqs, lambda i, a: (signal(barrier, d, (s + i) % seqs), a)[1], 0)

    @pl.when(owner == c)
    def _():
        pl.semaphore_wait(barrier, 2 * seqs - 1 + xs - 1)

    @pl.when(owner != c)
    def _():
        pl.semaphore_wait(barrier, 2 * seqs + xs - 1)

    columns = head_columns(head)

    span = NY * tokens
    my_columns = head_columns(y)

    def send_g(i, carry):
        r = (i + s) % rows_z
        to = (c * rows_z + r) * NY + z // NC
        src = grad.at[pl.ds(pl.multiple_of(r * span, span), span), :]
        dst = grads.at[x, :, my_columns]
        here = jnp.logical_and(owner == c, to == s)

        @pl.when(here)
        def _():
            pltpu.make_async_copy(src, dst, g_recv).start()

        @pl.when(jnp.logical_not(here))
        def _():
            remote(src, dst, g_send, g_recv, doc, to).start()

        return carry

    lax.fori_loop(0, rows_z, send_g, 0)

    def send_o(i, carry):
        r = (i + s) % half
        to = c * half + r
        src = att.at[pl.ds(pl.multiple_of(r * tokens, tokens), tokens), :]
        dst = att_o.at[:, columns]
        here = jnp.logical_and(owner == c, to == s)

        @pl.when(here)
        def _():
            pltpu.make_async_copy(src, dst, o_recv).start()

        @pl.when(jnp.logical_not(here))
        def _():
            remote(src, dst, o_send, o_recv, doc, to).start()

        return carry

    lax.fori_loop(0, half, send_o, 0)

    g_rows = gatt.shape[0]
    g_dst = gatt_o.at[pl.ds(pl.multiple_of(c * g_rows, g_rows), g_rows), columns]

    def send_n(i, carry):
        to = (i + s) % seqs
        here = jnp.logical_and(owner == c, i == 0)

        @pl.when(here)
        def _():
            pltpu.make_async_copy(gatt, g_dst, n_recv).start()

        @pl.when(jnp.logical_not(here))
        def _():
            remote(gatt, g_dst, n_send, n_recv, doc, to).start()

        return carry

    lax.fori_loop(0, seqs, send_n, 0)

    def arrived(ref, sem):
        pltpu.make_async_copy(ref, ref, sem).wait()

    arrived(grads.at[x], g_recv)
    for i in range(1, xs):
        to = (x + i) % xs
        remote(grads.at[x], grads.at[x], x_send.at[i - 1], x_recv.at[i - 1], to * NC + c, s).start()
    load.wait()
    depth = NY * tokens

    def product(source):
        lhs = f_v[pl.ds(pl.multiple_of(source * depth, depth), depth), :]
        return lax.dot_general(
            lhs, grads[source], (((0,), (0,)), ((), ())), preferred_element_type=jnp.float32
        )

    total[...] = product(x)
    for i in (1, xs - 1, *range(2, xs - 1)):
        if i >= xs or (i == xs - 1 and i == 1 and xs != 2):
            continue
        source = (x - i + xs) % xs
        arrived(grads.at[source], x_recv.at[i - 1])
        total[...] += product(source)
        if xs == 2:
            break

    rows = part.shape[0]
    other = total.at[pl.ds(pl.multiple_of((1 - c) * rows, rows), rows), :]
    remote(other, from_sibling, s_send, s_recv, sibling, s).start()
    arrived(from_sibling, s_recv)
    part[...] = total[pl.ds(pl.multiple_of(c * rows, rows), rows), :] + from_sibling[...]

    out_rows = w_o.shape[0]

    def send_w(i, carry):
        to = (i + s) % seqs
        src = part.at[pl.ds(pl.multiple_of(to * out_rows, out_rows), out_rows), :]
        remote(src, pieces.at[s], w_send, w_recv, d, to).start()
        return carry

    src = part.at[pl.ds(pl.multiple_of(s * out_rows, out_rows), out_rows), :]
    pltpu.make_async_copy(src, pieces.at[s], w_recv).start()
    lax.fori_loop(1, seqs, send_w, 0)
    arrived(pieces, w_recv)
    group = part.shape[1]
    for n in range(NY):
        acc = pieces[n]
        for m in range(1, seqs // NY):
            acc = acc + pieces[m * NY + n]
        w_o[:, n * group : (n + 1) * group] = acc

    arrived(att_o, o_recv)
    arrived(gatt_o, n_recv)

    @pl.when(mine)
    def _():
        arrived(att.at[pl.ds(0, (half - 1) * tokens), :], o_send)

    @pl.when(jnp.logical_not(mine))
    def _():
        arrived(att, o_send)

    mine_g = jnp.logical_and(mine, y == z // NC)

    @pl.when(mine_g)
    def _():
        arrived(grad.at[pl.ds(0, (rows_z - 1) * span), :], g_send)

    @pl.when(jnp.logical_not(mine_g))
    def _():
        arrived(grad, g_send)

    stand_in = gatt_o.at[pl.ds(0, g_rows), :]

    @pl.when(owner == c)
    def _():
        whole = att_o.shape[1] // E
        arrived(stand_in, n_send)
        arrived(gatt_o.at[pl.ds(0, g_rows), pl.ds(0, (whole - 1) * E)], n_send)

    @pl.when(owner != c)
    def _():
        arrived(gatt_o, n_send)

    for i in range(1, xs):
        arrived(grads.at[x], x_send.at[i - 1])
    arrived(from_sibling, s_send)
    arrived(pieces.at[pl.ds(0, seqs - 1)], w_send)


def product(seqs, xs, att, grad, gatt, f, wide, rows):
    tokens = att.shape[0] // (seqs // 2)
    hd = (seqs // 2) * E
    group = hd // NY
    shape = jax.ShapeDtypeStruct
    dma = pltpu.SemaphoreType.DMA
    f = f.reshape(-1, f.shape[2])
    return pl.pallas_call(
        functools.partial(product_kernel, seqs, xs),
        out_shape=(
            shape((tokens, hd), jnp.bfloat16),
            shape((gatt.shape[0] * NC, hd), jnp.bfloat16),
            shape((rows, hd), jnp.float32),
        ),
        in_specs=[ANY] * 4,
        out_specs=[ANY, ANY, pl.BlockSpec(memory_space=pltpu.VMEM)],
        scratch_shapes=[
            pltpu.VMEM(f.shape, jnp.bfloat16),
            pltpu.VMEM((xs, NY * tokens, group), jnp.bfloat16),
            pltpu.VMEM((wide // xs, group), jnp.float32),
            pltpu.VMEM((wide // xs // NC, group), jnp.float32),
            pltpu.VMEM((wide // xs // NC, group), jnp.float32),
            pltpu.VMEM((seqs, rows, group), jnp.float32),
            dma, dma, dma, dma, dma, dma, dma((xs - 1,)), dma((xs - 1,)),
            dma, dma, dma, dma, dma,
        ],
        compiler_params=pltpu.CompilerParams(
            collective_id=1, has_side_effects=True, vmem_limit_bytes=40 << 20
        ),
        name="product",
    )(att, grad, gatt, f)


def per_device(seqs, xs, features, queries, key_rows, value_rows, cotangent,
               global_queries, global_keys, global_values, random_blocks):
    wide = features.shape[2]
    q, k, v, g, f, gq, gk, gv, rb = shuffle(
        seqs, xs, queries, key_rows, value_rows, cotangent, features,
        global_queries, global_keys, global_values, random_blocks,
    )
    att, grad, gatt = attention(q, k, v, g, gq, gk, gv, rb)
    rows = wide // (seqs * xs * NC)
    attended, global_attended, weight_grad = product(seqs, xs, att, grad, gatt, f, wide, rows)
    return attended[None], global_attended[None], weight_grad


def solution(mesh):
    seqs, xs = mesh.shape["seq"], mesh.shape["dp"] // NC
    long, whole = P("dp", "seq", None), P("dp", None, None)
    return jax.shard_map(
        functools.partial(per_device, seqs, xs),
        mesh=mesh,
        in_specs=(long,) * 5 + (whole,) * 4,
        out_specs=(long, whole, P(("dp", "seq"), None)),
        check_vma=False,
    )
```

```python
import functools
import math

import jax
import jax.numpy as jnp
from jax import lax
from jax.experimental import pallas as pl
from jax.experimental.pallas import tpu as pltpu
from jax.sharding import PartitionSpec as P

E = 128
BLOCK = 64
R = 3
NY = 4
NC = 2
NEGATIVE = -1e30
MESH = pl.DeviceIdType.MESH
ANY = pl.BlockSpec(memory_space=pl.ANY)


def place(seqs):
    d, s = lax.axis_index("dp"), lax.axis_index("seq")
    return d, s, d // NC, d % NC, s // NY, s % NY


def head_columns(h):
    return pl.ds(pl.multiple_of(h * E, E), E)


def remote(src, dst, send, recv, d, s):
    return pltpu.make_async_remote_copy(
        src_ref=src, dst_ref=dst, send_sem=send, recv_sem=recv, device_id=(d, s), device_id_type=MESH
    )


def signal(sem, d, s):
    pl.semaphore_signal(sem, inc=1, device_id=(d, s), device_id_type=MESH)


def arrived(ref, sem):
    pltpu.make_async_copy(ref, ref, sem).wait()


def span(i, size):
    return pl.ds(pl.multiple_of(i * size, size), size)


def flip(a, i):
    low = (a % 2 + i % 2) % 2
    high = (a // 2 + i // 2) % max(NY // 2, 1)
    return high * 2 + low


dot = functools.partial(lax.dot_general, preferred_element_type=jnp.float32)
NT = (((1,), (1,)), ((), ()))
NN = (((1,), (0,)), ((), ()))


def layer_kernel(seqs, xs, *refs):
    q, k, v, g, f, gq, gk, gv, rb = refs[:9]
    att_o, gatt_o, w_o = refs[9:12]
    (qs, ks, vs, gs, fs, gqs, gks, gvs, rbv, rbs,
     probs, long_weights, own_weights, mass, att, grad, gatt, grads, turned,
     total, sib_out, sib_in, part, pieces,
     a_send, a_recv, b_send, b_recv, f_send, f_recv, c_send, c_recv, r_sem,
     o_send, o_recv, g_send, g_recv, n_send, n_recv, x_send, x_recv,
     s_send, s_recv, w_send, w_recv) = refs[12:]
    d, s, x, c, z, y = place(seqs)
    half = seqs // 2
    heads = half
    rows_z = half // NY
    tokens = att_o.shape[0]
    side = s // half
    slot = s % half
    sibling = x * NC + (1 - c)
    owner = z % NC
    doc = x * NC + owner
    head = (z // NC) * NY + y
    mine = jnp.logical_and(owner == c, side == c)
    others = jnp.logical_not(mine)
    scaling = 1.0 / math.sqrt(E)

    barrier = pltpu.get_barrier_semaphore()

    def greet(i, carry):
        source = c * half + i

        @pl.when(jnp.logical_not(jnp.logical_and(owner == c, source == s)))
        def _():
            signal(barrier, doc, source)

        return carry

    lax.fori_loop(0, half, greet, 0)
    signal(barrier, sibling, s)

    def greet_f(i, carry):
        signal(barrier, ((x + i // NY) % xs) * NC + c, z * NY + (y + i) % NY)
        return carry

    lax.fori_loop(1, xs * NY, greet_f, 0)

    @pl.when(mine)
    def _():
        pl.semaphore_wait(barrier, half + xs * NY - 1)

    @pl.when(others)
    def _():
        pl.semaphore_wait(barrier, half + xs * NY)

    def spread(n, array, dst):
        def body(i, carry):
            h = (i + s) % heads
            to = ((h // NY) * NC + c) * NY + h % NY
            src = array.at[..., head_columns(h)]
            here = jnp.logical_and(mine, to == s)

            @pl.when(here)
            def _():
                pltpu.make_async_copy(src, dst, a_recv.at[n]).start()

            @pl.when(jnp.logical_not(here))
            def _():
                remote(src, dst, a_send.at[n], a_recv.at[n], x * NC + side, to).start()

            return carry

        lax.fori_loop(0, heads, body, 0)

    g_rows = gqs.shape[0]
    columns = head_columns(head)
    shared = (
        (gq.at[0, span(c, g_rows), columns], gq.at[0, span(1 - c, g_rows), columns], gqs),
        (gk.at[0, :, columns], gk.at[0, :, columns], gks),
        (gv.at[0, :, columns], gv.at[0, :, columns], gvs),
        (rb, rb, rbv),
    )

    own_blocks = tokens // BLOCK

    spread(0, k, ks.at[span(s, own_blocks)])
    spread(2, q, qs.at[span(slot, tokens), :])

    @pl.when(owner == c)
    def _():
        for n, (own, other, dst) in enumerate(shared):
            pltpu.make_async_copy(own, dst, c_recv.at[n]).start()
            remote(other, dst, c_send.at[n], c_recv.at[n], sibling, s).start()

    spread(1, v, vs.at[span(s, own_blocks)])
    spread(3, g, gs.at[span(slot, tokens), :])

    width = fs.shape[1]
    f_dst = fs.at[span(x * NY + y, tokens), :]

    def send_f(i, carry):
        to_x, to_y = (x + i // NY) % xs, (y + i) % NY
        src = f.at[0, :, span(to_x, width)]
        remote(src, f_dst, f_send, f_recv, to_x * NC + c, z * NY + to_y).start()
        return carry

    pltpu.make_async_copy(f.at[0, :, span(x, width)], f_dst, f_recv).start()
    lax.fori_loop(1, xs * NY, send_f, 0)

    for n, (_, _, dst) in enumerate(shared):
        arrived(dst, c_recv.at[n])
    pltpu.make_async_copy(rbv, rbs, r_sem).start()
    pltpu.make_async_copy(rbv, rbs, r_sem).wait()

    blocks = ks.shape[0]
    count = blocks // 2
    own_part, other_part = span(c, count), span(1 - c, count)

    def share(n, ref):
        arrived(ref.at[own_part], a_recv.at[n])
        remote(ref.at[own_part], ref.at[own_part], b_send.at[n], b_recv.at[n], sibling, s).start()

    share(0, ks)
    arrived(qs, a_recv.at[2])
    arrived(ks.at[other_part], b_recv.at[0])

    g_k, g_v = gks[...], gvs[...]
    width_k = probs.shape[1]

    def listed(ref, b, own):
        first = jnp.clip(b - 1, 0, blocks - 3)
        window = [ref[first + n] for n in range(3)]
        picks = [ref[rbs[n, 0, b]] for n in range(R)]
        return jnp.concatenate(window + picks + [own], axis=0)

    def forward(i, carry):
        b = c * count + i
        scores = dot(qs[span(i, BLOCK), :], listed(ks, b, g_k), NT) * scaling
        low = jnp.where(b == blocks - 1, BLOCK, 0)
        high = jnp.where(b == 0, 2 * BLOCK, 3 * BLOCK)
        column = lax.broadcasted_iota(jnp.int32, (BLOCK, width_k), 1)
        valid = (column >= low) & ((column < high) | (column >= 3 * BLOCK))
        scores = jnp.where(valid, scores, NEGATIVE)
        weights = jnp.exp(scores - jnp.max(scores, axis=-1, keepdims=True))
        probs[span(i, BLOCK), :] = weights / jnp.sum(weights, axis=-1, keepdims=True)
        return carry

    lax.fori_loop(0, count, forward, 0, unroll=4)

    g_q = gqs[...]
    long_scores = dot(g_q, ks[...].reshape(-1, E), NT) * scaling
    own_scores = dot(g_q, g_k, NT) * scaling
    peak = jnp.maximum(
        jnp.max(long_scores, axis=-1, keepdims=True), jnp.max(own_scores, axis=-1, keepdims=True)
    )
    long_scores = jnp.exp(long_scores - peak)
    own_scores = jnp.exp(own_scores - peak)
    mass[...] = jnp.sum(long_scores, axis=-1, keepdims=True) + jnp.sum(
        own_scores, axis=-1, keepdims=True
    )
    long_weights[...] = long_scores.astype(jnp.bfloat16)
    own_weights[...] = own_scores.astype(jnp.bfloat16)

    share(1, vs)
    arrived(gs, a_recv.at[3])
    arrived(vs.at[other_part], b_recv.at[1])

    per_chunk = count // NY
    deep = NY * tokens
    my_row = z % rows_z

    def backward(i, carry):
        b = c * count + i
        rows = span(i, BLOCK)
        values = listed(vs, b, g_v)
        p = probs[rows, :]
        g_b = gs[rows, :]
        attended = dot(p.astype(jnp.bfloat16), values, NN).astype(jnp.bfloat16)
        delta = jnp.sum(
            g_b.astype(jnp.float32) * attended.astype(jnp.float32), axis=-1, keepdims=True
        )
        dprobs = dot(g_b, values, NT)
        dscores = (p * (dprobs - delta)).astype(jnp.bfloat16)
        att[rows, :] = attended
        grad[rows, :] = (dot(dscores, listed(ks, b, g_k), NN) * scaling).astype(jnp.bfloat16)
        return carry

    def send_g(i):
        r = flip(y, i)
        to = (c * rows_z + r) * NY + z // NC
        src, dst = grad.at[span(r, deep), :], grads.at[x, i]
        here = jnp.logical_and(owner == c, to == s)

        @pl.when(here)
        def _():
            pltpu.make_async_copy(src, dst, g_recv.at[i]).start()

        @pl.when(jnp.logical_not(here))
        def _():
            remote(src, dst, g_send.at[i], g_recv.at[i], doc, to).start()

    def pass_on(i):
        arrived(grads.at[x, i], g_recv.at[i])
        for j in range(1, xs):
            remote(
                grads.at[x, i], grads.at[x, i], x_send.at[i, j - 1], x_recv.at[i, j - 1],
                ((x + j) % xs) * NC + c, s,
            ).start()

    for i in range(NY):
        first = flip(y, i) * per_chunk
        lax.fori_loop(
            0, per_chunk, lambda n, a, first=first: backward(first + n, a), 0, unroll=4
        )
        send_g(i)
        if i > 0:
            pass_on(i - 1)

    def send_o(i, carry):
        r = (i + s) % half
        to = c * half + r
        src, dst = att.at[span(r, tokens), :], att_o.at[:, columns]
        here = jnp.logical_and(owner == c, to == s)

        @pl.when(here)
        def _():
            pltpu.make_async_copy(src, dst, o_recv).start()

        @pl.when(jnp.logical_not(here))
        def _():
            remote(src, dst, o_send, o_recv, doc, to).start()

        return carry

    lax.fori_loop(0, half, send_o, 0)

    sums = dot(long_weights[...], vs[...].reshape(-1, E), NN) + dot(own_weights[...], g_v, NN)
    gatt[...] = (sums / mass[...]).astype(jnp.bfloat16)

    pass_on(NY - 1)

    g_dst = gatt_o.at[span(c, g_rows), columns]

    def send_n(i, carry):
        to = (i + s) % seqs
        here = jnp.logical_and(owner == c, i == 0)

        @pl.when(here)
        def _():
            pltpu.make_async_copy(gatt, g_dst, n_recv).start()

        @pl.when(jnp.logical_not(here))
        def _():
            remote(gatt, g_dst, n_send, n_recv, doc, to).start()

        return carry

    lax.fori_loop(0, seqs, send_n, 0)

    arrived(fs, f_recv)
    for i in range(xs):
        turned[i] = fs[i * deep : (i + 1) * deep, :].T

    pairs = NY // 2
    pair = 2 * E
    rows = sib_in.shape[1]
    bit = my_row % 2
    for p in range(pairs):
        for i in (2 * p, 2 * p + 1):
            for j in range(1, xs):
                arrived(grads.at[(x + xs - j) % xs, i], x_recv.at[i, j - 1])
        acc = None
        for source in range(xs):
            rhs = jnp.concatenate(
                [grads[source, 2 * p + bit], grads[source, 2 * p + 1 - bit]], axis=1
            )
            term = dot(turned[source], rhs, NN)
            acc = term if acc is None else acc + term
        total[p] = acc
        sib_out[p] = total[p, span(1 - c, rows), :].astype(jnp.bfloat16)
        remote(sib_out.at[p], sib_in.at[p], s_send.at[p], s_recv.at[p], sibling, s).start()

    out_rows = w_o.shape[0]
    for p in range(pairs):
        arrived(sib_in.at[p], s_recv.at[p])
        block = total[p, span(c, rows), :] + sib_in[p].astype(jnp.float32)
        part[p] = block.astype(jnp.bfloat16).reshape(seqs, out_rows, pair)
        place_p = (my_row // 2 + p) % pairs
        dst = pieces.at[place_p, s]
        pltpu.make_async_copy(part.at[p, s], dst, w_recv).start()

        def send_w(i, carry, p=p, dst=dst):
            to = (i + s) % seqs
            remote(part.at[p, to], dst, w_send, w_recv, d, to).start()
            return carry

        lax.fori_loop(1, seqs, send_w, 0)

    arrived(pieces, w_recv)
    for n in range(NY):
        for p in range(pairs):
            acc = pieces[p, n].astype(jnp.float32)
            for m in range(1, seqs // NY):
                acc = acc + pieces[p, m * NY + n].astype(jnp.float32)
            start = (n * pairs + p) * pair
            w_o[:, start : start + pair] = acc

    arrived(att_o, o_recv)
    arrived(gatt_o, n_recv)

    for n in range(4):
        @pl.when(mine)
        def _():
            arrived(qs.at[pl.ds(0, (half - 1) * tokens), :], a_send.at[n])

        @pl.when(others)
        def _():
            arrived(qs, a_send.at[n])
    for n, ref in enumerate((ks, vs)):
        arrived(ref.at[own_part], b_send.at[n])

    @pl.when(owner == c)
    def _():
        for n, (_, _, dst) in enumerate(shared):
            arrived(dst, c_send.at[n])

    arrived(fs.at[pl.ds(0, (xs * NY - 1) * tokens), :], f_send)

    for i in range(NY):
        to = (c * rows_z + flip(y, i)) * NY + z // NC

        @pl.when(jnp.logical_not(jnp.logical_and(owner == c, to == s)))
        def _():
            arrived(grads.at[x, i], g_send.at[i])

        for j in range(1, xs):
            arrived(grads.at[x, i], x_send.at[i, j - 1])

    @pl.when(mine)
    def _():
        arrived(att.at[pl.ds(0, (half - 1) * tokens), :], o_send)

    @pl.when(others)
    def _():
        arrived(att, o_send)

    @pl.when(owner == c)
    def _():
        arrived(att.at[pl.ds(0, (seqs - 1) * g_rows), :], n_send)

    @pl.when(owner != c)
    def _():
        arrived(att.at[pl.ds(0, seqs * g_rows), :], n_send)

    for p in range(pairs):
        arrived(sib_in.at[p], s_send.at[p])
    arrived(pieces.at[:, pl.ds(0, seqs - 1)], w_send)


def layer(seqs, xs, q, k, v, g, f, gq, gk, gv, rb):
    tokens, hd, wide = q.shape[1], q.shape[2], f.shape[2]
    half, globals_ = seqs // 2, gk.shape[1]
    rows = wide // (seqs * xs * NC)
    width, g_rows, pair = wide // xs, globals_ // NC, 2 * E
    pairs, deep, length = NY // 2, NY * tokens, seqs * tokens
    columns = 3 * BLOCK + R * BLOCK + globals_
    shape, vmem, dma = jax.ShapeDtypeStruct, pltpu.VMEM, pltpu.SemaphoreType.DMA
    bf16, f32 = jnp.bfloat16, jnp.float32
    rb = jnp.transpose(rb, (2, 0, 1))
    q, g = q[0], g[0]
    k, v = (a.reshape(-1, BLOCK, hd) for a in (k, v))
    return pl.pallas_call(
        functools.partial(layer_kernel, seqs, xs),
        out_shape=(
            shape((tokens, hd), bf16),
            shape((globals_, hd), bf16),
            shape((rows, hd), f32),
        ),
        in_specs=[ANY] * 9,
        out_specs=[ANY, ANY, pl.BlockSpec(memory_space=vmem)],
        scratch_shapes=[
            vmem((half * tokens, E), bf16),
            vmem((length // BLOCK, BLOCK, E), bf16),
            vmem((length // BLOCK, BLOCK, E), bf16),
            vmem((half * tokens, E), bf16),
            vmem((xs * NY * tokens, width), bf16),
            vmem((g_rows, E), bf16),
            vmem((globals_, E), bf16),
            vmem((globals_, E), bf16),
            vmem(rb.shape, jnp.int32),
            pltpu.SMEM(rb.shape, jnp.int32),
            vmem((half * tokens, columns), f32),
            vmem((g_rows, length), bf16),
            vmem((g_rows, globals_), bf16),
            vmem((g_rows, 1), f32),
            vmem((half * tokens, E), bf16),
            vmem((half * tokens, E), bf16),
            vmem((g_rows, E), bf16),
            vmem((xs, NY, deep, E), bf16),
            vmem((xs, width, deep), bf16),
            vmem((pairs, width, pair), f32),
            vmem((pairs, width // NC, pair), bf16),
            vmem((pairs, width // NC, pair), bf16),
            vmem((pairs, seqs, rows, pair), bf16),
            vmem((pairs, seqs, rows, pair), bf16),
            dma((4,)), dma((4,)), dma((2,)), dma((2,)), dma, dma, dma((4,)), dma((4,)), dma,
            dma, dma, dma((NY,)), dma((NY,)), dma, dma, dma((NY, xs - 1)), dma((NY, xs - 1)),
            dma((pairs,)), dma((pairs,)), dma, dma,
        ],
        compiler_params=pltpu.CompilerParams(
            collective_id=0, has_side_effects=True, vmem_limit_bytes=48 << 20
        ),
        name="layer",
    )(q, k, v, g, f, gq, gk, gv, rb)


def per_device(seqs, xs, features, queries, key_rows, value_rows, cotangent,
               global_queries, global_keys, global_values, random_blocks):
    attended, global_attended, weight_grad = layer(
        seqs, xs, queries, key_rows, value_rows, cotangent, features,
        global_queries, global_keys, global_values, random_blocks,
    )
    return attended[None], global_attended[None], weight_grad


def solution(mesh):
    seqs, xs = mesh.shape["seq"], mesh.shape["dp"] // NC
    long, whole = P("dp", "seq", None), P("dp", None, None)
    return jax.shard_map(
        functools.partial(per_device, seqs, xs),
        mesh=mesh,
        in_specs=(long,) * 5 + (whole,) * 4,
        out_specs=(long, whole, P(("dp", "seq"), None)),
        check_vma=False,
    )
```

```python
import functools
import math

import jax
import jax.numpy as jnp
from jax import lax
from jax.experimental import pallas as pl
from jax.experimental.pallas import tpu as pltpu
from jax.sharding import PartitionSpec as P

E = 128
BLOCK = 64
R = 3
NY = 4
NC = 2
NEGATIVE = -1e30
MESH = pl.DeviceIdType.MESH
HBM = pl.BlockSpec(memory_space=pltpu.HBM)


def place(seqs):
    d, s = lax.axis_index("dp"), lax.axis_index("seq")
    return d, s, d // NC, d % NC, s // NY, s % NY


def head_columns(h):
    return pl.ds(pl.multiple_of(h * E, E), E)


def remote(src, dst, send, recv, d, s):
    return pltpu.make_async_remote_copy(
        src_ref=src, dst_ref=dst, send_sem=send, recv_sem=recv, device_id=(d, s), device_id_type=MESH
    )


def signal(sem, d, s):
    pl.semaphore_signal(sem, inc=1, device_id=(d, s), device_id_type=MESH)


def arrived(ref, sem):
    pltpu.make_async_copy(ref, ref, sem).wait()


def span(i, size):
    return pl.ds(pl.multiple_of(i * size, size), size)


def flip(a, i):
    low = (a % 2 + i % 2) % 2
    high = (a // 2 + i // 2) % max(NY // 2, 1)
    return high * 2 + low


dot = functools.partial(lax.dot_general, preferred_element_type=jnp.float32)
NT = (((1,), (1,)), ((), ()))
NN = (((1,), (0,)), ((), ()))


def layer_kernel(seqs, xs, *refs):
    q, k, v, g, f, gq, gk, gv, rb = refs[:9]
    att_o, gatt_o, w_o = refs[9:12]
    (qs, ks, vs, gs, fs, gqs, gks, gvs, rbv, rbs,
     probs, long_weights, own_weights, mass, att, grad, gatt, grads, turned,
     total, sib_out, sib_in, x_out, x_in, part, pieces,
     a_send, a_recv, b_send, b_recv, f_send, f_recv, c_send, c_recv, r_sem,
     o_send, o_recv, g_send, g_recv, n_send, n_recv, x_send, x_recv,
     s_send, s_recv, w_send, w_recv) = refs[12:]
    d, s, x, c, z, y = place(seqs)
    half = seqs // 2
    heads = half
    rows_z = half // NY
    tokens = att_o.shape[0]
    side = s // half
    slot = s % half
    sibling = x * NC + (1 - c)
    owner = z % NC
    doc = x * NC + owner
    head = (z // NC) * NY + y
    mine = jnp.logical_and(owner == c, side == c)
    others = jnp.logical_not(mine)
    scaling = 1.0 / math.sqrt(E)

    barrier = pltpu.get_barrier_semaphore()

    def greet(i, carry):
        source = c * half + i

        @pl.when(jnp.logical_not(jnp.logical_and(owner == c, source == s)))
        def _():
            signal(barrier, doc, source)

        return carry

    lax.fori_loop(0, half, greet, 0)
    signal(barrier, sibling, s)

    for i in range(1, NY):
        signal(barrier, d, z * NY + (y + i) % NY)
    for i in range(1, xs):
        signal(barrier, ((x + i) % xs) * NC + c, s)
    greeted = half + 1 + NY - 1 + xs - 1

    @pl.when(mine)
    def _():
        pl.semaphore_wait(barrier, greeted - 1)

    @pl.when(others)
    def _():
        pl.semaphore_wait(barrier, greeted)

    def spread(n, array, dst):
        def body(i, carry):
            h = (i + s) % heads
            to = ((h // NY) * NC + c) * NY + h % NY
            src = array.at[..., head_columns(h)]
            here = jnp.logical_and(mine, to == s)

            @pl.when(here)
            def _():
                pltpu.make_async_copy(src, dst, a_recv.at[n]).start()

            @pl.when(jnp.logical_not(here))
            def _():
                remote(src, dst, a_send.at[n], a_recv.at[n], x * NC + side, to).start()

            return carry

        lax.fori_loop(0, heads, body, 0)

    g_rows = gqs.shape[0]
    columns = head_columns(head)
    shared = (
        (gq.at[0, span(c, g_rows), columns], gq.at[0, span(1 - c, g_rows), columns], gqs),
        (gk.at[0, :, columns], gk.at[0, :, columns], gks),
        (gv.at[0, :, columns], gv.at[0, :, columns], gvs),
        (rb, rb, rbv),
    )

    own_blocks = tokens // BLOCK

    spread(0, k, ks.at[span(s, own_blocks)])
    spread(2, q, qs.at[span(slot, tokens), :])

    @pl.when(owner == c)
    def _():
        for n, (own, other, dst) in enumerate(shared):
            pltpu.make_async_copy(own, dst, c_recv.at[n]).start()
            remote(other, dst, c_send.at[n], c_recv.at[n], sibling, s).start()

    spread(1, v, vs.at[span(s, own_blocks)])
    spread(3, g, gs.at[span(slot, tokens), :])

    f_dst = fs.at[span(y, tokens), :]
    pltpu.make_async_copy(f, f_dst, f_recv).start()
    for i in range(1, NY):
        remote(f, f_dst, f_send, f_recv, d, z * NY + (y + i) % NY).start()

    for n, (_, _, dst) in enumerate(shared):
        arrived(dst, c_recv.at[n])
    pltpu.make_async_copy(rbv, rbs, r_sem).start()
    pltpu.make_async_copy(rbv, rbs, r_sem).wait()

    blocks = ks.shape[0]
    count = blocks // 2
    own_part, other_part = span(c, count), span(1 - c, count)

    def share(n, ref):
        arrived(ref.at[own_part], a_recv.at[n])
        remote(ref.at[own_part], ref.at[own_part], b_send.at[n], b_recv.at[n], sibling, s).start()

    share(0, ks)
    arrived(qs, a_recv.at[2])
    arrived(ks.at[other_part], b_recv.at[0])

    g_k, g_v = gks[...], gvs[...]
    width_k = probs.shape[1]

    def listed(ref, b, own):
        first = jnp.clip(b - 1, 0, blocks - 3)
        window = [ref[first + n] for n in range(3)]
        picks = [ref[rbs[n, 0, b]] for n in range(R)]
        return jnp.concatenate(window + picks + [own], axis=0)

    def forward(i, carry):
        b = c * count + i
        scores = dot(qs[span(i, BLOCK), :], listed(ks, b, g_k), NT) * scaling
        low = jnp.where(b == blocks - 1, BLOCK, 0)
        high = jnp.where(b == 0, 2 * BLOCK, 3 * BLOCK)
        column = lax.broadcasted_iota(jnp.int32, (BLOCK, width_k), 1)
        valid = (column >= low) & ((column < high) | (column >= 3 * BLOCK))
        scores = jnp.where(valid, scores, NEGATIVE)
        weights = jnp.exp(scores - jnp.max(scores, axis=-1, keepdims=True))
        probs[span(i, BLOCK), :] = weights / jnp.sum(weights, axis=-1, keepdims=True)
        return carry

    lax.fori_loop(0, count, forward, 0, unroll=4)

    g_q = gqs[...]
    long_scores = dot(g_q, ks[...].reshape(-1, E), NT) * scaling
    own_scores = dot(g_q, g_k, NT) * scaling
    peak = jnp.maximum(
        jnp.max(long_scores, axis=-1, keepdims=True), jnp.max(own_scores, axis=-1, keepdims=True)
    )
    long_scores = jnp.exp(long_scores - peak)
    own_scores = jnp.exp(own_scores - peak)
    mass[...] = jnp.sum(long_scores, axis=-1, keepdims=True) + jnp.sum(
        own_scores, axis=-1, keepdims=True
    )
    long_weights[...] = long_scores.astype(jnp.bfloat16)
    own_weights[...] = own_scores.astype(jnp.bfloat16)

    share(1, vs)
    arrived(gs, a_recv.at[3])
    arrived(vs.at[other_part], b_recv.at[1])

    per_chunk = count // NY
    deep = NY * tokens
    my_row = z % rows_z

    def backward(i, carry):
        b = c * count + i
        rows = span(i, BLOCK)
        values = listed(vs, b, g_v)
        p = probs[rows, :]
        g_b = gs[rows, :]
        attended = dot(p.astype(jnp.bfloat16), values, NN).astype(jnp.bfloat16)
        delta = jnp.sum(
            g_b.astype(jnp.float32) * attended.astype(jnp.float32), axis=-1, keepdims=True
        )
        dprobs = dot(g_b, values, NT)
        dscores = (p * (dprobs - delta)).astype(jnp.bfloat16)
        att[rows, :] = attended
        grad[rows, :] = (dot(dscores, listed(ks, b, g_k), NN) * scaling).astype(jnp.bfloat16)
        return carry

    def send_g(i):
        r = flip(y, i)
        to = (c * rows_z + r) * NY + z // NC
        src, dst = grad.at[span(r, deep), :], grads.at[i]
        here = jnp.logical_and(owner == c, to == s)

        @pl.when(here)
        def _():
            pltpu.make_async_copy(src, dst, g_recv.at[i]).start()

        @pl.when(jnp.logical_not(here))
        def _():
            remote(src, dst, g_send.at[i], g_recv.at[i], doc, to).start()

    for i in range(NY):
        first = flip(y, i) * per_chunk
        lax.fori_loop(
            0, per_chunk, lambda n, a, first=first: backward(first + n, a), 0, unroll=4
        )
        send_g(i)

    def send_o(i, carry):
        r = (i + s) % half
        to = c * half + r
        src, dst = att.at[span(r, tokens), :], att_o.at[:, columns]
        here = jnp.logical_and(owner == c, to == s)

        @pl.when(here)
        def _():
            pltpu.make_async_copy(src, dst, o_recv).start()

        @pl.when(jnp.logical_not(here))
        def _():
            remote(src, dst, o_send, o_recv, doc, to).start()

        return carry

    lax.fori_loop(0, half, send_o, 0)

    sums = dot(long_weights[...], vs[...].reshape(-1, E), NN) + dot(own_weights[...], g_v, NN)
    gatt[...] = (sums / mass[...]).astype(jnp.bfloat16)

    g_dst = gatt_o.at[span(c, g_rows), columns]

    def send_n(i, carry):
        to = (i + s) % seqs
        here = jnp.logical_and(owner == c, i == 0)

        @pl.when(here)
        def _():
            pltpu.make_async_copy(gatt, g_dst, n_recv).start()

        @pl.when(jnp.logical_not(here))
        def _():
            remote(gatt, g_dst, n_send, n_recv, doc, to).start()

        return carry

    lax.fori_loop(0, seqs, send_n, 0)

    arrived(fs, f_recv)
    step = turned.shape[0] // NY
    for i in range(NY):
        turned[i * step : (i + 1) * step, :] = fs[:, i * step : (i + 1) * step].T

    pairs = NY // 2
    pair = 2 * E
    rows = sib_in.shape[2]
    bit = my_row % 2
    for p in range(pairs):
        for i in (2 * p, 2 * p + 1):
            arrived(grads.at[i], g_recv.at[i])
        rhs = jnp.concatenate([grads[2 * p + bit], grads[2 * p + 1 - bit]], axis=1)
        for i in range(xs):
            slab = turned[i * NC * rows : (i + 1) * NC * rows, :]
            total[p, i] = dot(slab, rhs, NN)
            sib_out[p, i] = total[p, i, span(1 - c, rows), :].astype(jnp.bfloat16)
        remote(sib_out.at[p], sib_in.at[p], s_send.at[p], s_recv.at[p], sibling, s).start()

    def chip_sum(p, i):
        return total[p, i, span(c, rows), :] + sib_in[p, i].astype(jnp.float32)

    for p in range(pairs):
        arrived(sib_in.at[p], s_recv.at[p])
        for j in (*range(2, xs), 1)[: xs - 1]:
            to = (x + j) % xs
            x_out[p, j - 1] = chip_sum(p, to).astype(jnp.bfloat16)
            remote(
                x_out.at[p, j - 1], x_in.at[p, j - 1], x_send.at[p, j - 1], x_recv.at[p, j - 1],
                to * NC + c, s,
            ).start()

    out_rows = w_o.shape[0]
    for p in range(pairs):
        block = chip_sum(p, x)
        for j in range(1, xs):
            arrived(x_in.at[p, j - 1], x_recv.at[p, j - 1])
            block = block + x_in[p, j - 1].astype(jnp.float32)
        part[p] = block.astype(jnp.bfloat16).reshape(seqs, out_rows, pair)
        place_p = (my_row // 2 + p) % pairs
        dst = pieces.at[place_p, s]
        pltpu.make_async_copy(part.at[p, s], dst, w_recv).start()

        def send_w(i, carry, p=p, dst=dst):
            to = (i + s) % seqs
            remote(part.at[p, to], dst, w_send, w_recv, d, to).start()
            return carry

        lax.fori_loop(1, seqs, send_w, 0)

    arrived(pieces, w_recv)
    for n in range(NY):
        for p in range(pairs):
            acc = pieces[p, n].astype(jnp.float32)
            for m in range(1, seqs // NY):
                acc = acc + pieces[p, m * NY + n].astype(jnp.float32)
            start = (n * pairs + p) * pair
            w_o[:, start : start + pair] = acc

    arrived(att_o, o_recv)
    arrived(gatt_o, n_recv)

    for n in range(4):
        @pl.when(mine)
        def _():
            arrived(qs.at[pl.ds(0, (half - 1) * tokens), :], a_send.at[n])

        @pl.when(others)
        def _():
            arrived(qs, a_send.at[n])
    for n, ref in enumerate((ks, vs)):
        arrived(ref.at[own_part], b_send.at[n])

    @pl.when(owner == c)
    def _():
        for n, (_, _, dst) in enumerate(shared):
            arrived(dst, c_send.at[n])

    arrived(fs.at[pl.ds(0, (NY - 1) * tokens), :], f_send)

    for i in range(NY):
        to = (c * rows_z + flip(y, i)) * NY + z // NC

        @pl.when(jnp.logical_not(jnp.logical_and(owner == c, to == s)))
        def _():
            arrived(grads.at[i], g_send.at[i])

    @pl.when(mine)
    def _():
        arrived(att.at[pl.ds(0, (half - 1) * tokens), :], o_send)

    @pl.when(others)
    def _():
        arrived(att, o_send)

    @pl.when(owner == c)
    def _():
        arrived(att.at[pl.ds(0, (seqs - 1) * g_rows), :], n_send)

    @pl.when(owner != c)
    def _():
        arrived(att.at[pl.ds(0, seqs * g_rows), :], n_send)

    for p in range(pairs):
        arrived(sib_in.at[p], s_send.at[p])
        for j in range(1, xs):
            arrived(x_in.at[p, j - 1], x_send.at[p, j - 1])
    arrived(pieces.at[:, pl.ds(0, seqs - 1)], w_send)


def layer(seqs, xs, q, k, v, g, f, gq, gk, gv, rb):
    tokens, hd, wide = q.shape[1], q.shape[2], f.shape[2]
    half, globals_ = seqs // 2, gk.shape[1]
    rows = wide // (seqs * xs * NC)
    share, g_rows, pair = wide // (xs * NC), globals_ // NC, 2 * E
    pairs, deep, length = NY // 2, NY * tokens, seqs * tokens
    columns = 3 * BLOCK + R * BLOCK + globals_
    shape, vmem, dma = jax.ShapeDtypeStruct, pltpu.VMEM, pltpu.SemaphoreType.DMA
    bf16, f32 = jnp.bfloat16, jnp.float32
    rb = jnp.transpose(rb, (2, 0, 1))
    q, g, f = q[0], g[0], f[0]
    k, v = (a.reshape(-1, BLOCK, hd) for a in (k, v))
    return pl.pallas_call(
        functools.partial(layer_kernel, seqs, xs),
        out_shape=(
            shape((tokens, hd), bf16),
            shape((globals_, hd), bf16),
            shape((rows, hd), f32),
        ),
        in_specs=[HBM] * 9,
        out_specs=[HBM, HBM, pl.BlockSpec(memory_space=vmem)],
        scratch_shapes=[
            vmem((half * tokens, E), bf16),
            vmem((length // BLOCK, BLOCK, E), bf16),
            vmem((length // BLOCK, BLOCK, E), bf16),
            vmem((half * tokens, E), bf16),
            vmem((deep, wide), bf16),
            vmem((g_rows, E), bf16),
            vmem((globals_, E), bf16),
            vmem((globals_, E), bf16),
            vmem(rb.shape, jnp.int32),
            pltpu.SMEM(rb.shape, jnp.int32),
            vmem((half * tokens, columns), f32),
            vmem((g_rows, length), bf16),
            vmem((g_rows, globals_), bf16),
            vmem((g_rows, 1), f32),
            vmem((half * tokens, E), bf16),
            vmem((half * tokens, E), bf16),
            vmem((g_rows, E), bf16),
            vmem((NY, deep, E), bf16),
            vmem((wide, deep), bf16),
            vmem((pairs, xs, NC * share, pair), f32),
            vmem((pairs, xs, share, pair), bf16),
            vmem((pairs, xs, share, pair), bf16),
            vmem((pairs, xs - 1, share, pair), bf16),
            vmem((pairs, xs - 1, share, pair), bf16),
            vmem((pairs, seqs, rows, pair), bf16),
            vmem((pairs, seqs, rows, pair), bf16),
            dma((4,)), dma((4,)), dma((2,)), dma((2,)), dma, dma, dma((4,)), dma((4,)), dma,
            dma, dma, dma((NY,)), dma((NY,)), dma, dma, dma((pairs, xs - 1)), dma((pairs, xs - 1)),
            dma((pairs,)), dma((pairs,)), dma, dma,
        ],
        compiler_params=pltpu.CompilerParams(
            collective_id=0, has_side_effects=True, vmem_limit_bytes=56 << 20
        ),
        name="layer",
    )(q, k, v, g, f, gq, gk, gv, rb)


def per_device(seqs, xs, features, queries, key_rows, value_rows, cotangent,
               global_queries, global_keys, global_values, random_blocks):
    attended, global_attended, weight_grad = layer(
        seqs, xs, queries, key_rows, value_rows, cotangent, features,
        global_queries, global_keys, global_values, random_blocks,
    )
    return attended[None], global_attended[None], weight_grad


def solution(mesh):
    seqs, xs = mesh.shape["seq"], mesh.shape["dp"] // NC
    long, whole = P("dp", "seq", None), P("dp", None, None)
    return jax.shard_map(
        functools.partial(per_device, seqs, xs),
        mesh=mesh,
        in_specs=(long,) * 5 + (whole,) * 4,
        out_specs=(long, whole, P(("dp", "seq"), None)),
        check_vma=False,
    )
```

```python
import functools
import math

import jax
import jax.numpy as jnp
from jax import lax
from jax.experimental import pallas as pl
from jax.experimental.pallas import tpu as pltpu
from jax.sharding import PartitionSpec as P

E = 128
BLOCK = 64
R = 3
NY = 4
NC = 2
NEGATIVE = -1e30
MESH = pl.DeviceIdType.MESH
HBM = pl.BlockSpec(memory_space=pltpu.HBM)


def place(seqs):
    d, s = lax.axis_index("dp"), lax.axis_index("seq")
    return d, s, d // NC, d % NC, s // NY, s % NY


def head_columns(h):
    return pl.ds(pl.multiple_of(h * E, E), E)


def remote(src, dst, send, recv, d, s):
    return pltpu.make_async_remote_copy(
        src_ref=src, dst_ref=dst, send_sem=send, recv_sem=recv, device_id=(d, s), device_id_type=MESH
    )


def signal(sem, d, s):
    pl.semaphore_signal(sem, inc=1, device_id=(d, s), device_id_type=MESH)


def arrived(ref, sem):
    pltpu.make_async_copy(ref, ref, sem).wait()


def span(i, size):
    return pl.ds(pl.multiple_of(i * size, size), size)


def flip(a, i):
    low = (a % 2 + i % 2) % 2
    high = (a // 2 + i // 2) % max(NY // 2, 1)
    return high * 2 + low


dot = functools.partial(lax.dot_general, preferred_element_type=jnp.float32)
NT = (((1,), (1,)), ((), ()))
NN = (((1,), (0,)), ((), ()))


def layer_kernel(seqs, xs, *refs):
    q, k, v, g, f, gq, gk, gv, rb = refs[:9]
    att_o, gatt_o, w_o = refs[9:12]
    (qs, ks, vs, gs, fs, gqs, gks, gvs, rbv, rbs,
     probs, dscores, long_weights, own_weights, mass, att, grad, gatt, grads, turned,
     total, sib_out, sib_in, x_out, x_in, part, pieces,
     a_send, a_recv, b_send, b_recv, f_send, f_recv, c_send, c_recv, r_sem,
     o_send, o_recv, g_send, g_recv, n_send, n_recv, m_send, m_recv, x_send, x_recv,
     s_send, s_recv, w_send, w_recv) = refs[12:]
    d, s, x, c, z, y = place(seqs)
    half = seqs // 2
    heads = half
    rows_z = half // NY
    tokens = att_o.shape[0]
    side = s // half
    slot = s % half
    sibling = x * NC + (1 - c)
    owner = z % NC
    doc = x * NC + owner
    head = (z // NC) * NY + y
    mine = jnp.logical_and(owner == c, side == c)
    others = jnp.logical_not(mine)
    scaling = 1.0 / math.sqrt(E)

    barrier = pltpu.get_barrier_semaphore()

    def greet(i, carry):
        source = c * half + i

        @pl.when(jnp.logical_not(jnp.logical_and(owner == c, source == s)))
        def _():
            signal(barrier, doc, source)

        return carry

    lax.fori_loop(0, half, greet, 0)
    signal(barrier, sibling, s)

    for i in range(1, NY):
        signal(barrier, d, z * NY + (y + i) % NY)
    for i in range(1, xs):
        signal(barrier, ((x + i) % xs) * NC + c, s)
    greeted = half + 1 + NY - 1 + xs - 1

    @pl.when(mine)
    def _():
        pl.semaphore_wait(barrier, greeted - 1)

    @pl.when(others)
    def _():
        pl.semaphore_wait(barrier, greeted)

    def send_slice(n, array, dst, sem, h):
        to = ((h // NY) * NC + c) * NY + h % NY
        src = array.at[..., head_columns(h)]
        here = jnp.logical_and(mine, to == s)

        @pl.when(here)
        def _():
            pltpu.make_async_copy(src, dst, sem).start()

        @pl.when(jnp.logical_not(here))
        def _():
            remote(src, dst, a_send.at[n], sem, x * NC + side, to).start()

    def sent(n, few, count_all, count_few):
        few = jnp.logical_and(mine, few)

        @pl.when(few)
        def _():
            arrived(qs.at[pl.ds(0, count_few * tokens), :], a_send.at[n])

        @pl.when(jnp.logical_not(few))
        def _():
            arrived(qs.at[pl.ds(0, count_all * tokens), :], a_send.at[n])

    part_heads = heads // 2

    def spread(n, m, array, dst):
        def body(i, carry):
            send_slice(2 * n + m, array, dst, a_recv.at[n, 0], (i + s) % heads)
            return carry

        lax.fori_loop(m * part_heads, (m + 1) * part_heads, body, 0)

    def spread_sent(n, m):
        own = ((head + heads - s % heads) % heads) // part_heads
        sent(2 * n + m, own == m, part_heads, part_heads - 1)

    g_rows = gqs.shape[0]
    columns = head_columns(head)
    shared = (
        (gq.at[0, span(c, g_rows), columns], gq.at[0, span(1 - c, g_rows), columns], gqs),
        (gk.at[0, :, columns], gk.at[0, :, columns], gks),
        (gv.at[0, :, columns], gv.at[0, :, columns], gvs),
        (rb, rb, rbv),
    )

    own_blocks = tokens // BLOCK
    k_dst, v_dst = ks.at[span(s, own_blocks)], vs.at[span(s, own_blocks)]
    spread(0, 0, k, k_dst)
    spread(0, 1, k, k_dst)

    @pl.when(owner == c)
    def _():
        for n, (own, other, dst) in enumerate(shared):
            pltpu.make_async_copy(own, dst, c_recv.at[n]).start()
            remote(other, dst, c_send.at[n], c_recv.at[n], sibling, s).start()

    my_row = z % rows_z

    def spread_step(i):
        to_y = flip(my_row, i)

        def body(n, carry):
            h = ((n + z) % (heads // NY)) * NY + to_y
            send_slice(4 + i, q, qs.at[span(slot, tokens), :], a_recv.at[2, i], h)
            send_slice(4 + i, g, gs.at[span(slot, tokens), :], a_recv.at[3, i], h)
            return carry

        lax.fori_loop(0, heads // NY, body, 0)

    def step_sent(i):
        pieces_all = 2 * (heads // NY)
        sent(4 + i, flip(my_row, i) == y, pieces_all, pieces_all - 2)

    for m in range(2):
        spread(1, m, v, v_dst)
    spread_sent(0, 0)
    spread_step(0)
    spread_sent(0, 1)
    spread_step(1)

    f_dst = fs.at[span(y, tokens), :]
    pltpu.make_async_copy(f, f_dst, f_recv).start()
    for i in range(1, NY):
        remote(f, f_dst, f_send, f_recv, d, z * NY + (y + i) % NY).start()

    for n, (_, _, dst) in enumerate(shared):
        arrived(dst, c_recv.at[n])
    pltpu.make_async_copy(rbv, rbs, r_sem).start()
    pltpu.make_async_copy(rbv, rbs, r_sem).wait()

    blocks = ks.shape[0]
    count = blocks // 2
    own_part, other_part = span(c, count), span(1 - c, count)

    def share(n, ref):
        arrived(ref.at[own_part], a_recv.at[n, 0])
        remote(ref.at[own_part], ref.at[own_part], b_send.at[n], b_recv.at[n], sibling, s).start()

    share(0, ks)
    spread_sent(1, 0)
    if NY > 2:
        spread_step(2)
    arrived(ks.at[other_part], b_recv.at[0])

    g_k, g_v = gks[...], gvs[...]
    width_k = probs.shape[1]
    per_chunk = count // NY
    deep = NY * tokens

    def listed(ref, b, own):
        first = jnp.clip(b - 1, 0, blocks - 3)
        window = [ref[first + n] for n in range(3)]
        picks = [ref[rbs[n, 0, b]] for n in range(R)]
        return jnp.concatenate(window + picks + [own], axis=0)

    def forward(i, carry):
        b = c * count + i
        scores = dot(qs[span(i, BLOCK), :], listed(ks, b, g_k), NT) * scaling
        low = jnp.where(b == blocks - 1, BLOCK, 0)
        high = jnp.where(b == 0, 2 * BLOCK, 3 * BLOCK)
        column = lax.broadcasted_iota(jnp.int32, (BLOCK, width_k), 1)
        valid = (column >= low) & ((column < high) | (column >= 3 * BLOCK))
        scores = jnp.where(valid, scores, NEGATIVE)
        weights = jnp.exp(scores - jnp.max(scores, axis=-1, keepdims=True))
        probs[span(i % per_chunk, BLOCK), :] = weights / jnp.sum(weights, axis=-1, keepdims=True)
        return carry

    g_q = gqs[...]
    long_scores = dot(g_q, ks[...].reshape(-1, E), NT) * scaling
    own_scores = dot(g_q, g_k, NT) * scaling
    peak = jnp.maximum(
        jnp.max(long_scores, axis=-1, keepdims=True), jnp.max(own_scores, axis=-1, keepdims=True)
    )
    long_scores = jnp.exp(long_scores - peak)
    own_scores = jnp.exp(own_scores - peak)
    mass[...] = jnp.sum(long_scores, axis=-1, keepdims=True) + jnp.sum(
        own_scores, axis=-1, keepdims=True
    )
    long_weights[...] = long_scores.astype(jnp.bfloat16)
    own_weights[...] = own_scores.astype(jnp.bfloat16)

    spread_sent(1, 1)
    if NY > 3:
        spread_step(3)
    share(1, vs)
    arrived(vs.at[other_part], b_recv.at[1])
    sums = dot(long_weights[...], vs[...].reshape(-1, E), NN) + dot(own_weights[...], g_v, NN)
    gatt[...] = (sums / mass[...]).astype(jnp.bfloat16)

    g_dst = gatt_o.at[span(c, g_rows), columns]
    rows_all = seqs // NY

    @pl.when(owner == c)
    def _():
        pltpu.make_async_copy(gatt, g_dst, n_recv).start()

    @pl.when(owner != c)
    def _():
        remote(gatt, g_dst, n_send, n_recv, doc, s).start()

    for i in range(1, rows_all):
        remote(gatt, g_dst, n_send, n_recv, doc, ((z + i) % rows_all) * NY + y).start()


    def middle(i, carry):
        b = c * count + i
        rows, low_rows = span(i, BLOCK), span(i % per_chunk, BLOCK)
        values = listed(vs, b, g_v)
        p = probs[low_rows, :]
        g_b = gs[rows, :]
        dprobs = dot(g_b, values, NT)
        attended = dot(p.astype(jnp.bfloat16), values, NN).astype(jnp.bfloat16)
        delta = jnp.sum(
            g_b.astype(jnp.float32) * attended.astype(jnp.float32), axis=-1, keepdims=True
        )
        att[rows, :] = attended
        dscores[low_rows, :] = (p * (dprobs - delta)).astype(jnp.bfloat16)
        return carry

    def backward(i, carry):
        ds = dscores[span(i % per_chunk, BLOCK), :]
        product = dot(ds, listed(ks, c * count + i, g_k), NN)
        grad[span(i, BLOCK), :] = (product * scaling).astype(jnp.bfloat16)
        return carry

    def send_g(i):
        r = flip(y, i)
        to = (c * rows_z + r) * NY + z // NC
        src, dst = grad.at[span(r, deep), :], grads.at[i]
        here = jnp.logical_and(owner == c, to == s)

        @pl.when(here)
        def _():
            pltpu.make_async_copy(src, dst, g_recv.at[i]).start()

        @pl.when(jnp.logical_not(here))
        def _():
            remote(src, dst, g_send.at[i], g_recv.at[i], doc, to).start()

    def send_o(i, carry):
        r = (i + s) % half
        to = c * half + r
        src, dst = att.at[span(r, tokens), :], att_o.at[:, columns]
        here = jnp.logical_and(owner == c, to == s)

        @pl.when(here)
        def _():
            pltpu.make_async_copy(src, dst, o_recv).start()

        @pl.when(jnp.logical_not(here))
        def _():
            remote(src, dst, o_send, o_recv, doc, to).start()

        return carry

    def chunk(i):
        r = flip(y, i)
        arrived(qs.at[span(r, deep), :], a_recv.at[2, i])
        arrived(gs.at[span(r, deep), :], a_recv.at[3, i])
        for step in (forward, middle, backward):
            lax.fori_loop(
                0, per_chunk, lambda n, a, step=step: step(r * per_chunk + n, a), 0, unroll=True
            )
        send_g(i)

    pairs = NY // 2
    pair = 2 * E
    rows = sib_in.shape[2]
    bit = my_row % 2

    def turn():
        arrived(fs, f_recv)
        size = turned.shape[0] // NY
        for i in range(NY):
            turned[i * size : (i + 1) * size, :] = fs[:, i * size : (i + 1) * size].T

    def product(p):
        for i in (2 * p, 2 * p + 1):
            arrived(grads.at[i], g_recv.at[i])
        rhs = jnp.concatenate([grads[2 * p + bit], grads[2 * p + 1 - bit]], axis=1)
        for i in range(xs):
            slab = turned[i * NC * rows : (i + 1) * NC * rows, :]
            total[p, i] = dot(slab, rhs, NN)
            sib_out[p, i] = total[p, i, span(1 - c, rows), :].astype(jnp.bfloat16)
        remote(sib_out.at[p], sib_in.at[p], s_send.at[p], s_recv.at[p], sibling, s).start()

    def chip_sum(p, i):
        return total[p, i, span(c, rows), :] + sib_in[p, i].astype(jnp.float32)

    def along_x(p):
        arrived(sib_in.at[p], s_recv.at[p])
        for j in (*range(2, xs), 1)[: xs - 1]:
            to = (x + j) % xs
            x_out[p, j - 1] = chip_sum(p, to).astype(jnp.bfloat16)
            remote(
                x_out.at[p, j - 1], x_in.at[p, j - 1], x_send.at[p, j - 1], x_recv.at[p, j - 1],
                to * NC + c, s,
            ).start()

    out_rows = w_o.shape[0]

    def scatter(p):
        block = chip_sum(p, x)
        for j in range(1, xs):
            arrived(x_in.at[p, j - 1], x_recv.at[p, j - 1])
            block = block + x_in[p, j - 1].astype(jnp.float32)
        part[p] = block.astype(jnp.bfloat16).reshape(seqs, out_rows, pair)
        dst = pieces.at[(my_row // 2 + p) % pairs, s]
        pltpu.make_async_copy(part.at[p, s], dst, w_recv).start()

        def send_w(i, carry):
            to = (i + s) % seqs
            remote(part.at[p, to], dst, w_send, w_recv, d, to).start()
            return carry

        lax.fori_loop(1, seqs, send_w, 0)

    for i in range(NY - 1):
        chunk(i)
    if pairs > 1:
        turn()
        product(0)
    chunk(NY - 1)
    if pairs > 1:
        along_x(0)
    else:
        turn()

    group = att_o.shape[1] // NY
    arrived(gatt_o.at[:, pl.ds(0, group)], n_recv)
    for n in range(heads // NY):
        ref = gatt_o.at[:, head_columns(n * NY + y)]
        for i in range(1, NY):
            remote(ref, ref, m_send, m_recv, d, z * NY + (y + i) % NY).start()

    product(pairs - 1)
    lax.fori_loop(0, half, send_o, 0)
    if pairs > 1:
        scatter(0)
    along_x(pairs - 1)
    scatter(pairs - 1)

    arrived(pieces, w_recv)
    for n in range(NY):
        for p in range(pairs):
            acc = pieces[p, n].astype(jnp.float32)
            for m in range(1, seqs // NY):
                acc = acc + pieces[p, m * NY + n].astype(jnp.float32)
            start = (n * pairs + p) * pair
            w_o[:, start : start + pair] = acc

    arrived(att_o, o_recv)
    arrived(gatt_o.at[:, pl.ds(0, (NY - 1) * group)], m_recv)

    for i in range(NY):
        step_sent(i)
    for n, ref in enumerate((ks, vs)):
        arrived(ref.at[own_part], b_send.at[n])

    @pl.when(owner == c)
    def _():
        for n, (_, _, dst) in enumerate(shared):
            arrived(dst, c_send.at[n])

    arrived(fs.at[pl.ds(0, (NY - 1) * tokens), :], f_send)

    for i in range(NY):
        to = (c * rows_z + flip(y, i)) * NY + z // NC

        @pl.when(jnp.logical_not(jnp.logical_and(owner == c, to == s)))
        def _():
            arrived(grads.at[i], g_send.at[i])

    @pl.when(mine)
    def _():
        arrived(att.at[pl.ds(0, (half - 1) * tokens), :], o_send)

    @pl.when(others)
    def _():
        arrived(att, o_send)

    @pl.when(owner == c)
    def _():
        arrived(att.at[pl.ds(0, (rows_all - 1) * g_rows), :], n_send)

    @pl.when(owner != c)
    def _():
        arrived(att.at[pl.ds(0, rows_all * g_rows), :], n_send)

    arrived(gatt_o.at[:, pl.ds(0, (NY - 1) * group)], m_send)
    for p in range(pairs):
        arrived(sib_in.at[p], s_send.at[p])
        for j in range(1, xs):
            arrived(x_in.at[p, j - 1], x_send.at[p, j - 1])
    arrived(pieces.at[:, pl.ds(0, seqs - 1)], w_send)


def layer(seqs, xs, q, k, v, g, f, gq, gk, gv, rb):
    tokens, hd, wide = q.shape[1], q.shape[2], f.shape[2]
    half, globals_ = seqs // 2, gk.shape[1]
    rows = wide // (seqs * xs * NC)
    share, g_rows, pair = wide // (xs * NC), globals_ // NC, 2 * E
    pairs, deep, length = NY // 2, NY * tokens, seqs * tokens
    columns = 3 * BLOCK + R * BLOCK + globals_
    shape, vmem, dma = jax.ShapeDtypeStruct, pltpu.VMEM, pltpu.SemaphoreType.DMA
    bf16, f32 = jnp.bfloat16, jnp.float32
    rb = jnp.transpose(rb, (2, 0, 1))
    q, g, f = q[0], g[0], f[0]
    k, v = (a.reshape(-1, BLOCK, hd) for a in (k, v))
    return pl.pallas_call(
        functools.partial(layer_kernel, seqs, xs),
        out_shape=(
            shape((tokens, hd), bf16),
            shape((globals_, hd), bf16),
            shape((rows, hd), f32),
        ),
        in_specs=[HBM] * 9,
        out_specs=[HBM, HBM, pl.BlockSpec(memory_space=vmem)],
        scratch_shapes=[
            vmem((half * tokens, E), bf16),
            vmem((length // BLOCK, BLOCK, E), bf16),
            vmem((length // BLOCK, BLOCK, E), bf16),
            vmem((half * tokens, E), bf16),
            vmem((deep, wide), bf16),
            vmem((g_rows, E), bf16),
            vmem((globals_, E), bf16),
            vmem((globals_, E), bf16),
            vmem(rb.shape, jnp.int32),
            pltpu.SMEM(rb.shape, jnp.int32),
            vmem((half * tokens // NY, columns), f32),
            vmem((half * tokens // NY, columns), bf16),
            vmem((g_rows, length), bf16),
            vmem((g_rows, globals_), bf16),
            vmem((g_rows, 1), f32),
            vmem((half * tokens, E), bf16),
            vmem((half * tokens, E), bf16),
            vmem((g_rows, E), bf16),
            vmem((NY, deep, E), bf16),
            vmem((wide, deep), bf16),
            vmem((pairs, xs, NC * share, pair), f32),
            vmem((pairs, xs, share, pair), bf16),
            vmem((pairs, xs, share, pair), bf16),
            vmem((pairs, xs - 1, share, pair), bf16),
            vmem((pairs, xs - 1, share, pair), bf16),
            vmem((pairs, seqs, rows, pair), bf16),
            vmem((pairs, seqs, rows, pair), bf16),
            dma((4 + NY,)), dma((4, NY)), dma((2,)), dma((2,)), dma, dma, dma((4,)), dma((4,)), dma,
            dma, dma, dma((NY,)), dma((NY,)), dma, dma, dma, dma, dma((pairs, xs - 1)), dma((pairs, xs - 1)),
            dma((pairs,)), dma((pairs,)), dma, dma,
        ],
        compiler_params=pltpu.CompilerParams(
            collective_id=0, has_side_effects=True, vmem_limit_bytes=56 << 20
        ),
        name="layer",
    )(q, k, v, g, f, gq, gk, gv, rb)


def deliver_kernel(*refs):
    count = (len(refs) - 1) // 2
    copies = [
        pltpu.make_async_copy(refs[n], refs[count + n], refs[-1].at[n]) for n in range(count)
    ]
    for copy in copies:
        copy.start()
    for copy in copies:
        copy.wait()


def deliver(*arrays):
    count = len(arrays)
    return pl.pallas_call(
        deliver_kernel,
        out_shape=[jax.ShapeDtypeStruct(a.shape, a.dtype) for a in arrays],
        in_specs=[HBM] * count,
        out_specs=[HBM] * count,
        scratch_shapes=[pltpu.SemaphoreType.DMA((count,))],
        compiler_params=pltpu.CompilerParams(vmem_limit_bytes=56 << 20),
        name="deliver",
    )(*arrays)


def per_device(seqs, xs, features, queries, key_rows, value_rows, cotangent,
               global_queries, global_keys, global_values, random_blocks):
    attended, global_attended, weight_grad = layer(
        seqs, xs, queries, key_rows, value_rows, cotangent, features,
        global_queries, global_keys, global_values, random_blocks,
    )
    attended, global_attended, weight_grad = deliver(attended, global_attended, weight_grad)
    return attended[None], global_attended[None], weight_grad


def solution(mesh):
    seqs, xs = mesh.shape["seq"], mesh.shape["dp"] // NC
    long, whole = P("dp", "seq", None), P("dp", None, None)
    return jax.shard_map(
        functools.partial(per_device, seqs, xs),
        mesh=mesh,
        in_specs=(long,) * 5 + (whole,) * 4,
        out_specs=(long, whole, P(("dp", "seq"), None)),
        check_vma=False,
    )
```

```python
import functools
import math

import jax
import jax.numpy as jnp
from jax import lax
from jax.experimental import pallas as pl
from jax.experimental.pallas import tpu as pltpu
from jax.sharding import PartitionSpec as P

E = 128
BLOCK = 64
R = 3
NY = 4
NC = 2
NEGATIVE = -1e30
MESH = pl.DeviceIdType.MESH
HBM = pl.BlockSpec(memory_space=pltpu.HBM)


def place(seqs):
    d, s = lax.axis_index("dp"), lax.axis_index("seq")
    return d, s, d // NC, d % NC, s // NY, s % NY


def head_columns(h):
    return pl.ds(pl.multiple_of(h * E, E), E)


def remote(src, dst, send, recv, d, s):
    return pltpu.make_async_remote_copy(
        src_ref=src, dst_ref=dst, send_sem=send, recv_sem=recv, device_id=(d, s), device_id_type=MESH
    )


def signal(sem, d, s):
    pl.semaphore_signal(sem, inc=1, device_id=(d, s), device_id_type=MESH)


def arrived(ref, sem):
    pltpu.make_async_copy(ref, ref, sem).wait()


def span(i, size):
    return pl.ds(pl.multiple_of(i * size, size), size)


def flip(a, i):
    low = (a % 2 + i % 2) % 2
    high = (a // 2 + i // 2) % max(NY // 2, 1)
    return high * 2 + low


dot = functools.partial(lax.dot_general, preferred_element_type=jnp.float32)
NT = (((1,), (1,)), ((), ()))
NN = (((1,), (0,)), ((), ()))


def layer_kernel(seqs, xs, *refs):
    q, k, v, g, f, gq, gk, gv, rb = refs[:9]
    att_o, gatt_o, w_o = refs[9:12]
    (qs, ks, vs, gs, fs, gqs, gks, gvs, rbv, rbs,
     probs, dscores, long_weights, own_weights, mass, att, grad, gatt, grads, turned,
     total, sib_out, sib_in, x_out, x_in, part, pieces,
     a_send, a_recv, b_send, b_recv, f_send, f_recv, c_send, c_recv, r_sem,
     o_send, o_recv, g_send, g_recv, n_send, n_recv, m_send, m_recv, x_send, x_recv,
     s_send, s_recv, w_send, w_recv) = refs[12:]
    d, s, x, c, z, y = place(seqs)
    half = seqs // 2
    heads = half
    rows_z = half // NY
    tokens = att_o.shape[0]
    side = s // half
    slot = s % half
    sibling = x * NC + (1 - c)
    owner = z % NC
    doc = x * NC + owner
    head = (z // NC) * NY + y
    mine = jnp.logical_and(owner == c, side == c)
    others = jnp.logical_not(mine)
    scaling = 1.0 / math.sqrt(E)

    barrier = pltpu.get_barrier_semaphore()

    def greet(i, carry):
        source = c * half + i

        @pl.when(jnp.logical_not(jnp.logical_and(owner == c, source == s)))
        def _():
            signal(barrier, doc, source)

        return carry

    lax.fori_loop(0, half, greet, 0)
    signal(barrier, sibling, s)

    for i in range(1, NY):
        signal(barrier, d, z * NY + (y + i) % NY)
    for i in range(1, xs):
        signal(barrier, ((x + i) % xs) * NC + c, s)
    greeted = half + 1 + NY - 1 + xs - 1

    @pl.when(mine)
    def _():
        pl.semaphore_wait(barrier, greeted - 1)

    @pl.when(others)
    def _():
        pl.semaphore_wait(barrier, greeted)

    def send_slice(n, array, dst, sem, h):
        to = ((h // NY) * NC + c) * NY + h % NY
        src = array.at[..., head_columns(h)]
        here = jnp.logical_and(mine, to == s)

        @pl.when(here)
        def _():
            pltpu.make_async_copy(src, dst, sem).start()

        @pl.when(jnp.logical_not(here))
        def _():
            remote(src, dst, a_send.at[n], sem, x * NC + side, to).start()

    def sent(n, few, count_all, count_few):
        few = jnp.logical_and(mine, few)

        @pl.when(few)
        def _():
            arrived(qs.at[pl.ds(0, count_few * tokens), :], a_send.at[n])

        @pl.when(jnp.logical_not(few))
        def _():
            arrived(qs.at[pl.ds(0, count_all * tokens), :], a_send.at[n])

    part_heads = heads // 2

    def spread(n, m, array, dst):
        def body(i, carry):
            send_slice(2 * n + m, array, dst, a_recv.at[n, 0], (i + s) % heads)
            return carry

        lax.fori_loop(m * part_heads, (m + 1) * part_heads, body, 0)

    def spread_sent(n, m):
        own = ((head + heads - s % heads) % heads) // part_heads
        sent(2 * n + m, own == m, part_heads, part_heads - 1)

    g_rows = gqs.shape[0]
    columns = head_columns(head)
    shared = (
        (gq.at[0, span(c, g_rows), columns], gq.at[0, span(1 - c, g_rows), columns], gqs),
        (gk.at[0, :, columns], gk.at[0, :, columns], gks),
        (gv.at[0, :, columns], gv.at[0, :, columns], gvs),
        (rb, rb, rbv),
    )

    own_blocks = tokens // BLOCK
    k_dst, v_dst = ks.at[span(s, own_blocks)], vs.at[span(s, own_blocks)]
    spread(0, 0, k, k_dst)
    spread(0, 1, k, k_dst)

    @pl.when(owner == c)
    def _():
        for n, (own, other, dst) in enumerate(shared):
            pltpu.make_async_copy(own, dst, c_recv.at[n]).start()
            remote(other, dst, c_send.at[n], c_recv.at[n], sibling, s).start()

    my_row = z % rows_z

    def spread_step(i):
        to_y = flip(my_row, i)

        def body(n, carry):
            h = ((n + z) % (heads // NY)) * NY + to_y
            send_slice(4 + i, q, qs.at[span(slot, tokens), :], a_recv.at[2, i], h)
            send_slice(4 + i, g, gs.at[span(slot, tokens), :], a_recv.at[3, i], h)
            return carry

        lax.fori_loop(0, heads // NY, body, 0)

    def step_sent(i):
        pieces_all = 2 * (heads // NY)
        sent(4 + i, flip(my_row, i) == y, pieces_all, pieces_all - 2)

    for m in range(2):
        spread(1, m, v, v_dst)
    spread_step(0)
    spread_sent(0, 0)
    spread_step(1)
    spread_sent(0, 1)

    f_dst = fs.at[span(y, tokens), :]
    pltpu.make_async_copy(f, f_dst, f_recv).start()
    for i in range(1, NY):
        remote(f, f_dst, f_send, f_recv, d, z * NY + (y + i) % NY).start()

    for n, (_, _, dst) in enumerate(shared):
        arrived(dst, c_recv.at[n])
    pltpu.make_async_copy(rbv, rbs, r_sem).start()
    pltpu.make_async_copy(rbv, rbs, r_sem).wait()

    blocks = ks.shape[0]
    count = blocks // 2
    own_part, other_part = span(c, count), span(1 - c, count)

    def share(n, ref):
        arrived(ref.at[own_part], a_recv.at[n, 0])
        remote(ref.at[own_part], ref.at[own_part], b_send.at[n], b_recv.at[n], sibling, s).start()

    share(0, ks)
    spread_sent(1, 0)
    if NY > 2:
        spread_step(2)
    arrived(ks.at[other_part], b_recv.at[0])

    g_k, g_v = gks[...], gvs[...]
    width_k = probs.shape[1]
    per_chunk = count // NY
    deep = NY * tokens

    def listed(ref, b, own):
        first = jnp.clip(b - 1, 0, blocks - 3)
        window = [ref[first + n] for n in range(3)]
        picks = [ref[rbs[n, 0, b]] for n in range(R)]
        return jnp.concatenate(window + picks + [own], axis=0)

    def forward(i, carry):
        b = c * count + i
        scores = dot(qs[span(i, BLOCK), :], listed(ks, b, g_k), NT) * scaling
        low = jnp.where(b == blocks - 1, BLOCK, 0)
        high = jnp.where(b == 0, 2 * BLOCK, 3 * BLOCK)
        column = lax.broadcasted_iota(jnp.int32, (BLOCK, width_k), 1)
        valid = (column >= low) & ((column < high) | (column >= 3 * BLOCK))
        scores = jnp.where(valid, scores, NEGATIVE)
        weights = jnp.exp(scores - jnp.max(scores, axis=-1, keepdims=True))
        probs[span(i % per_chunk, BLOCK), :] = weights / jnp.sum(weights, axis=-1, keepdims=True)
        return carry

    g_q = gqs[...]
    long_scores = dot(g_q, ks[...].reshape(-1, E), NT) * scaling
    own_scores = dot(g_q, g_k, NT) * scaling
    peak = jnp.maximum(
        jnp.max(long_scores, axis=-1, keepdims=True), jnp.max(own_scores, axis=-1, keepdims=True)
    )
    long_scores = jnp.exp(long_scores - peak)
    own_scores = jnp.exp(own_scores - peak)
    mass[...] = jnp.sum(long_scores, axis=-1, keepdims=True) + jnp.sum(
        own_scores, axis=-1, keepdims=True
    )
    long_weights[...] = long_scores.astype(jnp.bfloat16)
    own_weights[...] = own_scores.astype(jnp.bfloat16)

    spread_sent(1, 1)
    if NY > 3:
        spread_step(3)
    share(1, vs)
    arrived(vs.at[other_part], b_recv.at[1])
    sums = dot(long_weights[...], vs[...].reshape(-1, E), NN) + dot(own_weights[...], g_v, NN)
    gatt[...] = (sums / mass[...]).astype(jnp.bfloat16)

    g_dst = gatt_o.at[span(c, g_rows), columns]
    rows_all = seqs // NY

    @pl.when(owner == c)
    def _():
        pltpu.make_async_copy(gatt, g_dst, n_recv).start()

    @pl.when(owner != c)
    def _():
        remote(gatt, g_dst, n_send, n_recv, doc, s).start()

    for i in range(1, rows_all):
        remote(gatt, g_dst, n_send, n_recv, doc, ((z + i) % rows_all) * NY + y).start()


    def middle(i, carry):
        b = c * count + i
        rows, low_rows = span(i, BLOCK), span(i % per_chunk, BLOCK)
        values = listed(vs, b, g_v)
        p = probs[low_rows, :]
        g_b = gs[rows, :]
        dprobs = dot(g_b, values, NT)
        attended = dot(p.astype(jnp.bfloat16), values, NN).astype(jnp.bfloat16)
        delta = jnp.sum(
            g_b.astype(jnp.float32) * attended.astype(jnp.float32), axis=-1, keepdims=True
        )
        att[rows, :] = attended
        dscores[low_rows, :] = (p * (dprobs - delta)).astype(jnp.bfloat16)
        return carry

    def backward(i, carry):
        ds = dscores[span(i % per_chunk, BLOCK), :]
        product = dot(ds, listed(ks, c * count + i, g_k), NN)
        grad[span(i, BLOCK), :] = (product * scaling).astype(jnp.bfloat16)
        return carry

    def send_g(i):
        r = flip(y, i)
        to = (c * rows_z + r) * NY + z // NC
        src, dst = grad.at[span(r, deep), :], grads.at[i]
        here = jnp.logical_and(owner == c, to == s)

        @pl.when(here)
        def _():
            pltpu.make_async_copy(src, dst, g_recv.at[i]).start()

        @pl.when(jnp.logical_not(here))
        def _():
            remote(src, dst, g_send.at[i], g_recv.at[i], doc, to).start()

    def send_o(i, carry):
        r = (i + s) % half
        to = c * half + r
        src, dst = att.at[span(r, tokens), :], att_o.at[:, columns]
        here = jnp.logical_and(owner == c, to == s)

        @pl.when(here)
        def _():
            pltpu.make_async_copy(src, dst, o_recv).start()

        @pl.when(jnp.logical_not(here))
        def _():
            remote(src, dst, o_send, o_recv, doc, to).start()

        return carry

    def chunk(i):
        r = flip(y, i)
        arrived(qs.at[span(r, deep), :], a_recv.at[2, i])
        arrived(gs.at[span(r, deep), :], a_recv.at[3, i])
        for step in (forward, middle, backward):
            lax.fori_loop(
                0, per_chunk, lambda n, a, step=step: step(r * per_chunk + n, a), 0, unroll=True
            )
        send_g(i)

    pairs = NY // 2
    pair = 2 * E
    rows = sib_in.shape[2]
    bit = my_row % 2

    def turn():
        arrived(fs, f_recv)
        size = turned.shape[0] // NY
        for i in range(NY):
            turned[i * size : (i + 1) * size, :] = fs[:, i * size : (i + 1) * size].T

    def product(p):
        for i in (2 * p, 2 * p + 1):
            arrived(grads.at[i], g_recv.at[i])
        rhs = jnp.concatenate([grads[2 * p + bit], grads[2 * p + 1 - bit]], axis=1)
        for i in range(xs):
            slab = turned[i * NC * rows : (i + 1) * NC * rows, :]
            total[p, i] = dot(slab, rhs, NN)
            sib_out[p, i] = total[p, i, span(1 - c, rows), :].astype(jnp.bfloat16)
        remote(sib_out.at[p], sib_in.at[p], s_send.at[p], s_recv.at[p], sibling, s).start()

    def chip_sum(p, i):
        return total[p, i, span(c, rows), :] + sib_in[p, i].astype(jnp.float32)

    def along_x(p):
        arrived(sib_in.at[p], s_recv.at[p])
        for j in (*range(2, xs), 1)[: xs - 1]:
            to = (x + j) % xs
            x_out[p, j - 1] = chip_sum(p, to).astype(jnp.bfloat16)
            remote(
                x_out.at[p, j - 1], x_in.at[p, j - 1], x_send.at[p, j - 1], x_recv.at[p, j - 1],
                to * NC + c, s,
            ).start()

    out_rows = w_o.shape[0]

    def scatter(p):
        block = chip_sum(p, x)
        for j in range(1, xs):
            arrived(x_in.at[p, j - 1], x_recv.at[p, j - 1])
            block = block + x_in[p, j - 1].astype(jnp.float32)
        part[p] = block.astype(jnp.bfloat16).reshape(seqs, out_rows, pair)
        dst = pieces.at[(my_row // 2 + p) % pairs, s]
        pltpu.make_async_copy(part.at[p, s], dst, w_recv).start()

        def send_w(i, carry):
            to = (i + s) % seqs
            remote(part.at[p, to], dst, w_send, w_recv, d, to).start()
            return carry

        lax.fori_loop(1, seqs, send_w, 0)

    for i in range(NY - 1):
        chunk(i)
    if pairs > 1:
        turn()
        product(0)
    chunk(NY - 1)
    if pairs > 1:
        along_x(0)
    else:
        turn()

    group = att_o.shape[1] // NY
    arrived(gatt_o.at[:, pl.ds(0, group)], n_recv)
    for n in range(heads // NY):
        ref = gatt_o.at[:, head_columns(n * NY + y)]
        for i in range(1, NY):
            remote(ref, ref, m_send, m_recv, d, z * NY + (y + i) % NY).start()

    product(pairs - 1)
    lax.fori_loop(0, half, send_o, 0)
    if pairs > 1:
        scatter(0)
    along_x(pairs - 1)
    scatter(pairs - 1)

    arrived(pieces, w_recv)
    for n in range(NY):
        for p in range(pairs):
            acc = pieces[p, n].astype(jnp.float32)
            for m in range(1, seqs // NY):
                acc = acc + pieces[p, m * NY + n].astype(jnp.float32)
            start = (n * pairs + p) * pair
            w_o[:, start : start + pair] = acc

    arrived(att_o, o_recv)
    arrived(gatt_o.at[:, pl.ds(0, (NY - 1) * group)], m_recv)

    for i in range(NY):
        step_sent(i)
    for n, ref in enumerate((ks, vs)):
        arrived(ref.at[own_part], b_send.at[n])

    @pl.when(owner == c)
    def _():
        for n, (_, _, dst) in enumerate(shared):
            arrived(dst, c_send.at[n])

    arrived(fs.at[pl.ds(0, (NY - 1) * tokens), :], f_send)

    for i in range(NY):
        to = (c * rows_z + flip(y, i)) * NY + z // NC

        @pl.when(jnp.logical_not(jnp.logical_and(owner == c, to == s)))
        def _():
            arrived(grads.at[i], g_send.at[i])

    @pl.when(mine)
    def _():
        arrived(att.at[pl.ds(0, (half - 1) * tokens), :], o_send)

    @pl.when(others)
    def _():
        arrived(att, o_send)

    @pl.when(owner == c)
    def _():
        arrived(att.at[pl.ds(0, (rows_all - 1) * g_rows), :], n_send)

    @pl.when(owner != c)
    def _():
        arrived(att.at[pl.ds(0, rows_all * g_rows), :], n_send)

    arrived(gatt_o.at[:, pl.ds(0, (NY - 1) * group)], m_send)
    for p in range(pairs):
        arrived(sib_in.at[p], s_send.at[p])
        for j in range(1, xs):
            arrived(x_in.at[p, j - 1], x_send.at[p, j - 1])
    arrived(pieces.at[:, pl.ds(0, seqs - 1)], w_send)


def layer(seqs, xs, q, k, v, g, f, gq, gk, gv, rb):
    tokens, hd, wide = q.shape[1], q.shape[2], f.shape[2]
    half, globals_ = seqs // 2, gk.shape[1]
    rows = wide // (seqs * xs * NC)
    share, g_rows, pair = wide // (xs * NC), globals_ // NC, 2 * E
    pairs, deep, length = NY // 2, NY * tokens, seqs * tokens
    columns = 3 * BLOCK + R * BLOCK + globals_
    shape, vmem, dma = jax.ShapeDtypeStruct, pltpu.VMEM, pltpu.SemaphoreType.DMA
    bf16, f32 = jnp.bfloat16, jnp.float32
    rb = jnp.transpose(rb, (2, 0, 1))
    q, g, f = q[0], g[0], f[0]
    k, v = (a.reshape(-1, BLOCK, hd) for a in (k, v))
    return pl.pallas_call(
        functools.partial(layer_kernel, seqs, xs),
        out_shape=(
            shape((tokens, hd), bf16),
            shape((globals_, hd), bf16),
            shape((rows, hd), f32),
        ),
        in_specs=[HBM] * 9,
        out_specs=[HBM, HBM, pl.BlockSpec(memory_space=vmem)],
        scratch_shapes=[
            vmem((half * tokens, E), bf16),
            vmem((length // BLOCK, BLOCK, E), bf16),
            vmem((length // BLOCK, BLOCK, E), bf16),
            vmem((half * tokens, E), bf16),
            vmem((deep, wide), bf16),
            vmem((g_rows, E), bf16),
            vmem((globals_, E), bf16),
            vmem((globals_, E), bf16),
            vmem(rb.shape, jnp.int32),
            pltpu.SMEM(rb.shape, jnp.int32),
            vmem((half * tokens // NY, columns), f32),
            vmem((half * tokens // NY, columns), bf16),
            vmem((g_rows, length), bf16),
            vmem((g_rows, globals_), bf16),
            vmem((g_rows, 1), f32),
            vmem((half * tokens, E), bf16),
            vmem((half * tokens, E), bf16),
            vmem((g_rows, E), bf16),
            vmem((NY, deep, E), bf16),
            vmem((wide, deep), bf16),
            vmem((pairs, xs, NC * share, pair), f32),
            vmem((pairs, xs, share, pair), bf16),
            vmem((pairs, xs, share, pair), bf16),
            vmem((pairs, xs - 1, share, pair), bf16),
            vmem((pairs, xs - 1, share, pair), bf16),
            vmem((pairs, seqs, rows, pair), bf16),
            vmem((pairs, seqs, rows, pair), bf16),
            dma((4 + NY,)), dma((4, NY)), dma((2,)), dma((2,)), dma, dma, dma((4,)), dma((4,)), dma,
            dma, dma, dma((NY,)), dma((NY,)), dma, dma, dma, dma, dma((pairs, xs - 1)), dma((pairs, xs - 1)),
            dma((pairs,)), dma((pairs,)), dma, dma,
        ],
        compiler_params=pltpu.CompilerParams(
            collective_id=0, has_side_effects=True, vmem_limit_bytes=56 << 20
        ),
        name="layer",
    )(q, k, v, g, f, gq, gk, gv, rb)


def deliver_kernel(*refs):
    count = len(refs) // 2
    for n in range(count):
        refs[count + n][...] = refs[n][...]


def deliver(*arrays):
    vmem = pl.BlockSpec(memory_space=pltpu.VMEM)
    return pl.pallas_call(
        deliver_kernel,
        out_shape=[jax.ShapeDtypeStruct(a.shape, a.dtype) for a in arrays],
        in_specs=[vmem] * len(arrays),
        out_specs=[vmem] * len(arrays),
        compiler_params=pltpu.CompilerParams(vmem_limit_bytes=56 << 20),
        name="deliver",
    )(*arrays)


def per_device(seqs, xs, features, queries, key_rows, value_rows, cotangent,
               global_queries, global_keys, global_values, random_blocks):
    attended, global_attended, weight_grad = layer(
        seqs, xs, queries, key_rows, value_rows, cotangent, features,
        global_queries, global_keys, global_values, random_blocks,
    )
    attended, global_attended, weight_grad = deliver(attended, global_attended, weight_grad)
    return attended[None], global_attended[None], weight_grad


def solution(mesh):
    seqs, xs = mesh.shape["seq"], mesh.shape["dp"] // NC
    long, whole = P("dp", "seq", None), P("dp", None, None)
    return jax.shard_map(
        functools.partial(per_device, seqs, xs),
        mesh=mesh,
        in_specs=(long,) * 5 + (whole,) * 4,
        out_specs=(long, whole, P(("dp", "seq"), None)),
        check_vma=False,
    )
```
